256 devices in a mesh: blk: 32 (over z, y), rep: 8 (over x, core).
Axes of the slice: x: 4, y: 4, z: 8, core: 2. Of those that a mesh axis runs over, the one named last changes fastest.
Arguments:
- features: bfloat16 [16384, 1024], P('blk'), may hold values from -8 to 8
- node_order: int32 [16384], P('blk'), may hold values from 0 to 511, as said below
- adj_tiles: bfloat16 [32, 8, 4, 4, 256, 256], P('blk', 'rep'), may hold values from -0.0703125 to 0.1171875
- counts: int32 [32, 8, 4], P('blk', 'rep'), may hold values from 0 to 4, as said below
- coords: int32 [32, 8, 4, 4, 2], P('blk', 'rep'), may hold values from 0 to 1, as said below
- w_self: bfloat16 [1024, 1024], replicated, may hold values from -0.1875 to 0.1875
- w_neigh: bfloat16 [1024, 1024], replicated, may hold values from -0.1875 to 0.1875
- norm_gain: float32 [1024], P('rep'), may hold values from 0.5 to 1.5
- norm_bias: float32 [1024], P('rep'), may hold values from -0.5 to 0.5
- mean_scale: float32 [1024], P('rep'), may hold values from 0.2 to 1
- cotangent: bfloat16 [16384, 1024], P('blk', 'rep'), may hold values from -10 to 10
Outputs:
- normed: bfloat16 [16384, 1024], P('blk', 'rep')
- grad_feats: bfloat16 [16384, 1024], P(('blk', 'rep'))
- grad_neigh: float32 [1024, 1024], P('blk', 'rep')
- grad_norm: float32 [3, 1024], P(None, 'rep')
The draws below stay inside these ranges and needn't reach their ends.
Inputs may be any that keep to these rules, and one draw needn't show every extreme that they name: `node_order`: each aligned run of 512 entries holds every number 0 to 511 once. `counts`: in every draw some row block, replica and step has all 4 slots live. `coords`: the 4 pairs of row tile and column tile of one row block, replica and step are distinct.
All inputs are finite; a program needn't handle non-finite values.
Results may differ from the reference program's by a relative error of at most 0.017.
Values may be sent and summed in bfloat16 or wider, within the bound.
A program may use at most 128 MiB of HBM per device.

```python
import jax
import jax.numpy as jnp
from jax import lax

D = 1024
TILE = 256
SLOTS = 4
ROWS_BLK = 512
NODES = 16384
STEPS = 4
N_BLK = 32
N_REP = 8


def draw_features(key, part):
    key_noise, key_bias = jax.random.split(key)
    noise_draw = jnp.clip(jax.random.normal(key_noise, (NODES, D), jnp.float32), -5.0, 5.0)
    row_rise = 1.0 + 2.0 * jnp.arange(NODES, dtype=jnp.float32) / NODES
    col_bias = jax.random.uniform(key_bias, (D,), jnp.float32, -1.0, 1.0) * (3.2 * ROWS_BLK / (TILE * NODES ** 0.5))
    return (noise_draw + row_rise[:, None] * col_bias[None, :]).astype(jnp.bfloat16)


def draw_node_order(key, part):
    scores = jax.random.randint(key, (N_BLK, ROWS_BLK), 0, 1024) * ROWS_BLK + jnp.arange(ROWS_BLK, dtype=jnp.int32)[None, :]
    return jnp.argsort(scores, axis=1).astype(jnp.int32).reshape(NODES)


def draw_adj_tiles(key, part):
    tile_scale = 2.0 * ROWS_BLK / (TILE * NODES ** 0.5)

    def one_block(block_id):
        block_key = jax.random.fold_in(key, block_id)
        key_mask, key_value = jax.random.split(block_key)
        tile_shape = (N_REP, STEPS, SLOTS, TILE, TILE)
        present = jax.random.bernoulli(key_mask, 0.25, tile_shape)
        values = jax.random.uniform(key_value, tile_shape, jnp.float32, -1.0, 1.0) + 0.25
        row_rise = 1.0 + 2.0 * block_id.astype(jnp.float32) / N_BLK
        return (jnp.where(present, values, 0.0) * (row_rise * tile_scale)).astype(jnp.bfloat16)
    return lax.map(one_block, jnp.arange(N_BLK, dtype=jnp.int32))


def draw_counts(key, part):
    key_heavy, key_jitter, key_spot = jax.random.split(key, 3)
    is_heavy = jax.random.randint(key_heavy, (N_BLK, 1, 1), 0, 4) == 0
    base_level = jnp.where(is_heavy, SLOTS, 1)
    jitter = jax.random.randint(key_jitter, (N_BLK, N_REP, STEPS), -1, 2)
    tile_load = jnp.clip(base_level + jitter, 0, SLOTS).reshape(-1)
    full_spot = jax.random.randint(key_spot, (), 0, N_BLK * N_REP * STEPS)
    tile_load = tile_load.at[full_spot].set(SLOTS)
    return tile_load.reshape(N_BLK, N_REP, STEPS).astype(jnp.int32)


def draw_coords(key, part):
    tile_cols = ROWS_BLK // TILE
    positions = tile_cols * tile_cols
    scores = jax.random.randint(key, (N_BLK, N_REP, STEPS, positions), 0, 65536) * positions + jnp.arange(positions, dtype=jnp.int32)
    picked = jnp.argsort(scores, axis=-1)[..., :SLOTS].astype(jnp.int32)
    return jnp.stack([picked // tile_cols, picked % tile_cols], axis=-1).astype(jnp.int32)


def draw_cotangent(key, part):
    key_noise, key_bias = jax.random.split(key)
    noise_draw = jnp.clip(jax.random.normal(key_noise, (NODES, D), jnp.float32), -5.0, 5.0)
    row_rise = 1.0 + 2.0 * jnp.arange(NODES, dtype=jnp.float32) / NODES
    col_bias = jax.random.uniform(key_bias, (D,), jnp.float32, -0.5, 0.5)
    return (noise_draw + row_rise[:, None] * col_bias[None, :]).astype(jnp.bfloat16)


def shard_levels(stream_key, extent, pieces, least, largest):
    gain = 1.0
    for position, blocks in pieces:
        steps = jax.random.uniform(jax.random.fold_in(jax.random.fold_in(stream_key, 6), position), (blocks,), jnp.float32, least / len(pieces), largest / len(pieces))
        gain = gain * jnp.repeat(jnp.exp(steps), extent[position] // blocks).reshape((-1,) + (1,) * (len(extent) - 1 - position))
    return gain


def scatter_about(key, extent, spread, bound, kind=jnp.bfloat16):
    values = spread * jax.random.normal(key, extent, jnp.float32)
    return jnp.clip(values, min=-bound, max=bound).astype(kind)


def setup_inputs(seed: int = 0) -> dict:
    keys = jax.random.split(jax.random.key(seed), 12)
    features = draw_features(jax.random.fold_in(keys[11], 71), 0)
    node_order = draw_node_order(jax.random.fold_in(keys[11], 71), 0)
    adj_tiles = draw_adj_tiles(jax.random.fold_in(keys[11], 71), 0)
    counts = draw_counts(jax.random.fold_in(keys[11], 71), 0)
    coords = draw_coords(jax.random.fold_in(keys[11], 71), 0)
    w_self = scatter_about(keys[5], (D, D), D ** -0.5, 0.1875)
    w_neigh = scatter_about(keys[6], (D, D), D ** -0.5, 0.1875)
    norm_gain = jnp.clip(0.5 + 1.0 * jax.random.uniform(keys[7], (D,), jnp.float32) ** shard_levels(keys[7], (D,), ((0, 8),), -0.2, 0.2), 0.5, 1.5)
    norm_bias = jnp.clip(jax.random.uniform(keys[8], (D,), jnp.float32, -0.5, 0.5) * shard_levels(keys[8], (D,), ((0, 8),), -0.4, 0.0), -0.5, 0.5)
    mean_scale = jnp.clip(0.2 + 0.8 * jax.random.uniform(keys[9], (D,), jnp.float32) ** shard_levels(keys[9], (D,), ((0, 8),), -0.2, 0.2), 0.2, 1.0)
    cotangent = draw_cotangent(jax.random.fold_in(keys[11], 71), 0)
    return dict(features=features, node_order=node_order, adj_tiles=adj_tiles, counts=counts, coords=coords, w_self=w_self, w_neigh=w_neigh, norm_gain=norm_gain, norm_bias=norm_bias, mean_scale=mean_scale, cotangent=cotangent)


EPSILON = 1e-05
PRECISE = lax.Precision.HIGHEST

def reference(features, node_order, adj_tiles, counts, coords, w_self, w_neigh, norm_gain, norm_bias, mean_scale, cotangent):
    tile_cols = ROWS_BLK // TILE
    offsets = (jnp.arange(N_BLK, dtype=jnp.int32) * ROWS_BLK)[:, None]
    reordered = features[(node_order.reshape(N_BLK, ROWS_BLK) + offsets).reshape(-1)]
    rep_ids = jnp.arange(N_REP, dtype=jnp.int32)[:, None, None]
    step_ids = jnp.arange(STEPS, dtype=jnp.int32)[None, :, None]
    slot_ids = jnp.arange(SLOTS, dtype=jnp.int32)[None, None, :]
    feat_tiles = reordered.reshape(NODES // TILE, TILE, D)
    tile_ids = jnp.arange(tile_cols, dtype=jnp.int32)

    def slot_info(block_id):
        col_block = jnp.remainder(block_id - rep_ids - N_REP * step_ids, N_BLK)
        is_live = slot_ids < counts[block_id][:, :, None]
        col_tile = (col_block * tile_cols + coords[block_id][..., 1]).reshape(-1)
        row_tile = coords[block_id][..., 0].reshape(-1)
        return (is_live.reshape(-1), row_tile, col_tile)

    def agg_block(block_id):
        is_live, row_tile, col_tile = slot_info(block_id)
        blk_tiles = adj_tiles[block_id].reshape(-1, TILE, TILE).astype(jnp.float32)
        gathered = feat_tiles[col_tile].astype(jnp.float32)
        product = jnp.einsum('tab,tbd->tad', blk_tiles, gathered, precision=PRECISE)
        select = ((row_tile[None, :] == tile_ids[:, None]) & is_live[None, :]).astype(jnp.float32)
        block_out = jnp.einsum('qt,tad->qad', select, product, precision=PRECISE)
        return block_out.reshape(ROWS_BLK, D)
    aggregate = lax.map(agg_block, jnp.arange(N_BLK, dtype=jnp.int32)).reshape(NODES, D).astype(jnp.bfloat16)
    pre_norm = jnp.dot(reordered, w_self, preferred_element_type=jnp.float32) + jnp.dot(aggregate, w_neigh, preferred_element_type=jnp.float32)
    col_mean = lax.optimization_barrier(jnp.sum(pre_norm, axis=0)) / NODES
    centered = pre_norm - mean_scale * col_mean
    col_scale = jnp.sqrt(lax.optimization_barrier(jnp.sum(centered * centered, axis=0)) / NODES + EPSILON)
    normed = (norm_gain * centered / col_scale + norm_bias).astype(jnp.bfloat16)
    upstream = cotangent.astype(jnp.float32)
    cot_sum = lax.optimization_barrier(jnp.sum(upstream, axis=0))
    cot_cent = lax.optimization_barrier(jnp.sum(upstream * centered, axis=0))
    grad_centered = norm_gain * upstream / col_scale - centered * (norm_gain * cot_cent / (NODES * col_scale ** 3))
    grad_cent_total = norm_gain * cot_sum / col_scale - (1.0 - mean_scale) * col_mean * norm_gain * cot_cent / col_scale ** 3
    grad_pre = (grad_centered - mean_scale * grad_cent_total / NODES).astype(jnp.bfloat16)
    grad_agg = jnp.dot(grad_pre, w_neigh.T, preferred_element_type=jnp.float32).astype(jnp.bfloat16)
    self_part = jnp.dot(grad_pre, w_self.T, preferred_element_type=jnp.float32)
    grad_tiles = grad_agg.reshape(NODES // TILE, TILE, D)

    def back_block(carried, block_id):
        is_live, row_tile, col_tile = slot_info(block_id)
        blk_tiles = adj_tiles[block_id].reshape(-1, TILE, TILE).astype(jnp.float32)
        row_data = grad_tiles[block_id * tile_cols + row_tile].astype(jnp.float32)
        product = jnp.einsum('tab,tad->tbd', blk_tiles, row_data, precision=PRECISE)
        product = product * is_live.astype(jnp.float32)[:, None, None]
        return (carried.at[col_tile].add(product), None)
    start = jnp.zeros((NODES // TILE, TILE, D), jnp.float32)
    carried, unused = lax.scan(back_block, start, jnp.arange(N_BLK, dtype=jnp.int32))
    grad_feats = (self_part + carried.reshape(NODES, D)).astype(jnp.bfloat16)
    grad_neigh = jnp.dot(aggregate.T, grad_pre, preferred_element_type=jnp.float32) / NODES
    grad_norm = jnp.stack([cot_cent / col_scale, cot_sum, -col_mean * grad_cent_total]) / NODES
    return (normed, grad_feats, grad_neigh, grad_norm)
```

```python
import jax
import jax.numpy as jnp
from jax import lax
from jax.experimental import pallas as pl
from jax.experimental.pallas import tpu as pltpu
from jax.sharding import PartitionSpec as P

EPSILON = 1e-05
MESH = pl.DeviceIdType.MESH
NY = 4
NX = 4
BF16 = jnp.bfloat16
F32 = jnp.float32


def remote(src, dst, send_sem, recv_sem, blk, rep):
    return pltpu.make_async_remote_copy(
        src_ref=src,
        dst_ref=dst,
        send_sem=send_sem,
        recv_sem=recv_sem,
        device_id=(blk, rep),
        device_id_type=MESH,
    )


def greet(peers):
    barrier = pltpu.get_barrier_semaphore()
    for blk, rep in peers:
        pl.semaphore_signal(barrier, inc=1, device_id=(blk, rep), device_id_type=MESH)
    pl.semaphore_wait(barrier, len(peers))


class Place:
    def __init__(self):
        self.b = lax.axis_index("blk")
        self.r = lax.axis_index("rep")
        self.nb = lax.axis_size("blk")
        self.nr = lax.axis_size("rep")
        self.nz = self.nb // NY
        self.y = self.b % NY
        self.z = self.b // NY
        self.x = self.r // 2
        self.k = self.r % 2
        self.sib = self.x * 2 + (1 - self.k)

    def block(self, dy, dz):
        return ((self.z + dz + self.nz) % self.nz) * NY + (self.y + dy + NY) % NY

    def across(self, dx):
        return ((self.x + dx) % NX) * 2 + self.k

    def torus_peers(self):
        steps = ((1, 0), (-1, 0), (0, 1), (0, -1))
        return [(self.block(dy, dz), self.r) for dy, dz in steps]

    def rep_peers(self):
        return [(self.b, (self.r + d) % self.nr) for d in range(1, self.nr)]

    def line_peers(self):
        return [(self.b, self.across(d)) for d in range(1, NX)] + [(self.b, self.sib)]


DYS = (0, -1, 1, 2)


def gather_kernel(
    piece_ref,
    adj_ref,
    agg_ref,
    g,
    o,
    acc,
    pb,
    rb1,
    qb,
    rb2,
    piece_recv,
    half_recv,
    line_send,
    swap_send,
    swap_recv,
    own_sem,
    red_send,
    red_recv1,
    red_recv2,
    all_send,
    all_recv,
    sib_recv,
):
    at = Place()
    b, r, nr = at.b, at.r, at.nr
    rows = piece_ref.shape[0]
    half = rows // 2
    greet(at.torus_peers() + at.rep_peers())
    g[b] = piece_ref[...]

    def to_line(dyi, dz, dz_step):
        c = at.block(DYS[dyi], dz)
        target = (dz - dz_step) % at.nz
        remote(
            g.at[c], g.at[c], line_send, piece_recv.at[dyi, target], at.block(0, dz_step), r
        ).start()

    def hand_out(dyi, dz):
        c = at.block(DYS[dyi], dz)
        diff = (b - c + at.nb) % at.nb
        goal = diff % nr
        step = diff // nr

        @pl.when(goal != r)
        def _():
            remote(
                g.at[c], o.at[step, r], swap_send, swap_recv.at[step], b, goal
            ).start()

        @pl.when(goal == r)
        def _():
            pltpu.make_async_copy(g.at[c], o.at[step, r], own_sem.at[step]).start()

    def arrive(dyi, dz):
        c = at.block(DYS[dyi], dz)
        remote(
            g.at[c], g.at[c], line_send, piece_recv.at[dyi, dz % at.nz], b, r
        ).wait_recv()

    for dyi, dy in ((2, -1), (1, 1)):
        remote(
            g.at[b], g.at[b], line_send, piece_recv.at[1 if dy == 1 else 2, 0], at.block(dy, 0), r
        ).start()
    to_line(0, 0, 1)
    to_line(0, 0, -1)
    hand_out(0, 0)
    for dyi, onward, low in ((1, 1, 0), (2, -1, half)):
        arrive(dyi, 0)
        c = at.block(DYS[dyi], 0)
        part = pl.ds(low, half)
        remote(
            g.at[c, part], g.at[c, part], line_send, half_recv.at[dyi - 1], at.block(onward, 0), r
        ).start()
        to_line(dyi, 0, 1)
        to_line(dyi, 0, -1)
        hand_out(dyi, 0)
    far = at.block(2, 0)
    for i, low in ((0, 0), (1, half)):
        part = pl.ds(low, half)
        remote(
            g.at[far, part], g.at[far, part], line_send, half_recv.at[i], b, r
        ).wait_recv()
    to_line(3, 0, 1)
    to_line(3, 0, -1)
    hand_out(3, 0)
    reach = at.nz // 2
    for t in range(1, reach):
        for dyi in range(4):
            for way in (1, -1):
                dz = -t * way
                arrive(dyi, dz)
                if t < reach - 1 or (way == 1) == (dyi < 2):
                    to_line(dyi, dz, way)
                hand_out(dyi, dz)
    for dyi in (0, 2, 1, 3):
        arrive(dyi, reach)
        hand_out(dyi, reach)

    wide = acc.shape[1]
    tile = 256
    for i, step in enumerate((0, 1, 3, 2)):
        pltpu.make_async_copy(o.at[step, 0], o.at[step, 0], own_sem.at[step]).wait()
        some = o.at[step, pl.ds(0, nr - 1)]
        remote(some, some, swap_send, swap_recv.at[step], b, r).wait_recv()

        def tiles(n, carry, step=step, i=i):
            cols = pl.ds(pl.multiple_of(n * tile, tile), tile)
            source = o[step, :, :, cols].reshape(nr * rows, tile)
            out = jnp.dot(adj_ref[step], source, preferred_element_type=F32)
            acc[:, cols] = out if i == 0 else acc[:, cols] + out
            return carry

        lax.fori_loop(0, wide // tile, tiles, 0)

    x, k, sib = at.x, at.k, at.sib
    for m in range(NX):
        other = (1 - k) * NX + m
        part = acc[pl.ds(pl.multiple_of(other * rows, rows), rows), :]
        pb[m] = part.astype(BF16)
    remote(pb, rb1, red_send.at[0], red_recv1, b, sib).start()
    remote(pb, rb1, red_send.at[0], red_recv1, b, sib).wait_recv()
    for d in (2, 1, 3):
        goal = (x + d) % NX
        mine = k * NX + goal
        part = acc[pl.ds(pl.multiple_of(mine * rows, rows), rows), :]
        qb[d - 1] = (part + rb1[goal].astype(F32)).astype(BF16)
        remote(
            qb.at[d - 1], rb2.at[d - 1], red_send.at[d], red_recv2.at[d - 1], b, at.across(d)
        ).start()
    home = k * NX + x
    total = acc[pl.ds(pl.multiple_of(home * rows, rows), rows), :] + rb1[x].astype(F32)
    for d in (1, 3, 2):
        remote(
            qb.at[d - 1], rb2.at[d - 1], red_send.at[d], red_recv2.at[d - 1], b, at.across(d)
        ).wait_recv()
        total = total + rb2[d - 1].astype(F32)
    agg_ref[home] = total.astype(BF16)
    for d in (2, 1, 3):
        remote(
            agg_ref.at[home], agg_ref.at[home], all_send.at[d - 1], all_recv.at[d - 1], b, at.across(d)
        ).start()
    remote(
        agg_ref.at[home], agg_ref.at[home], all_send.at[3], sib_recv.at[0], b, sib
    ).start()
    for d in (1, 3, 2):
        came = k * NX + (x - d + NX) % NX
        remote(
            agg_ref.at[came], agg_ref.at[came], all_send.at[d - 1], all_recv.at[d - 1], b, sib
        ).wait_recv()
        remote(
            agg_ref.at[came], agg_ref.at[came], all_send.at[3 + d], sib_recv.at[d], b, sib
        ).start()
    for d in range(4):
        came = (1 - k) * NX + (x - d + NX) % NX
        remote(
            agg_ref.at[came], agg_ref.at[came], all_send.at[3], sib_recv.at[d], b, sib
        ).wait_recv()
    count = 3 + 4 * (at.nz - 1)
    some = g.at[pl.ds(0, count)]
    remote(some, some, line_send, piece_recv.at[0, 0], b, sib).wait_send()
    some = g.at[pl.ds(0, 4 * (nr - 1))]
    remote(some, some, swap_send, piece_recv.at[0, 0], b, sib).wait_send()
    remote(pb, rb1, red_send.at[0], red_recv1, b, sib).wait_send()
    for d in range(1, NX):
        remote(
            qb.at[d - 1], rb2.at[d - 1], red_send.at[d], red_recv2.at[d - 1], b, sib
        ).wait_send()
    for i in range(7):
        remote(
            agg_ref.at[home], agg_ref.at[home], all_send.at[i], sib_recv.at[0], b, sib
        ).wait_send()


def gather_features(piece, adj):
    rows, wide = piece.shape
    nb, nr = lax.axis_size("blk"), lax.axis_size("rep")
    dma = pltpu.SemaphoreType.DMA
    vmem = pl.BlockSpec(memory_space=pltpu.VMEM)
    return pl.pallas_call(
        gather_kernel,
        out_shape=jax.ShapeDtypeStruct((nr, rows, wide), BF16),
        in_specs=[vmem, vmem],
        out_specs=vmem,
        scratch_shapes=[
            pltpu.VMEM((nb, rows, wide), BF16),
            pltpu.VMEM((nb // nr, nr, rows, wide), BF16),
            pltpu.VMEM((nr * rows, wide), F32),
            pltpu.VMEM((NX, rows, wide), BF16),
            pltpu.VMEM((NX, rows, wide), BF16),
            pltpu.VMEM((NX - 1, rows, wide), BF16),
            pltpu.VMEM((NX - 1, rows, wide), BF16),
            dma((4, nb // NY)),
            dma((2,)),
            dma(()),
            dma(()),
            dma((4,)),
            dma((4,)),
            dma((4,)),
            dma(()),
            dma((3,)),
            dma((7,)),
            dma((3,)),
            dma((4,)),
        ],
        compiler_params=pltpu.CompilerParams(
            collective_id=0, has_side_effects=True, vmem_limit_bytes=48 << 20
        ),
        name="gather_features",
    )(piece, adj)


def stats_kernel(mine_ref, all_ref, send_sem, recv_sem):
    at = Place()
    b, r, nb = at.b, at.r, at.nb
    greet([((b + d) % nb, r) for d in range(1, nb)])
    for d in range(1, nb):
        remote(mine_ref, all_ref.at[b], send_sem, recv_sem, (b + d) % nb, r).start()
    all_ref[b] = mine_ref[...]
    some = all_ref.at[pl.ds(0, nb - 1)]
    remote(some, some, send_sem, recv_sem, b, at.sib).wait()


def share_stats(mine):
    nb = lax.axis_size("blk")
    vmem = pl.BlockSpec(memory_space=pltpu.VMEM)
    return pl.pallas_call(
        stats_kernel,
        out_shape=jax.ShapeDtypeStruct((nb,) + mine.shape, F32),
        in_specs=[vmem],
        out_specs=vmem,
        scratch_shapes=[pltpu.SemaphoreType.DMA(()), pltpu.SemaphoreType.DMA(())],
        compiler_params=pltpu.CompilerParams(collective_id=1, has_side_effects=True),
        name="share_stats",
    )(mine)


def columns_kernel(mine_ref, all_ref, send_sem, line_recv, sib_recv):
    at = Place()
    b, r, x, k, sib = at.b, at.r, at.x, at.k, at.sib
    width = mine_ref.shape[1]
    greet(at.line_peers())

    def cols(rep):
        return all_ref.at[:, pl.ds(pl.multiple_of(rep * width, width), width)]

    for d in (2, 1, 3):
        remote(mine_ref, cols(r), send_sem.at[d - 1], line_recv.at[d - 1], b, at.across(d)).start()
    remote(mine_ref, cols(r), send_sem.at[3], sib_recv.at[0], b, sib).start()
    all_ref[:, pl.ds(pl.multiple_of(r * width, width), width)] = mine_ref[...]
    for d in (1, 3, 2):
        came = cols(at.across(NX - d))
        remote(came, came, send_sem.at[d - 1], line_recv.at[d - 1], b, sib).wait_recv()
        remote(came, came, send_sem.at[3 + d], sib_recv.at[d], b, sib).start()
    for d in range(4):
        came = cols(((x - d + NX) % NX) * 2 + (1 - k))
        remote(came, came, send_sem.at[3], sib_recv.at[d], b, sib).wait_recv()
    for i in range(7):
        remote(mine_ref, mine_ref, send_sem.at[i], sib_recv.at[0], b, sib).wait_send()


def gather_columns(mine):
    rows, width = mine.shape
    nr = lax.axis_size("rep")
    dma = pltpu.SemaphoreType.DMA
    vmem = pl.BlockSpec(memory_space=pltpu.VMEM)
    return pl.pallas_call(
        columns_kernel,
        out_shape=jax.ShapeDtypeStruct((rows, width * nr), BF16),
        in_specs=[vmem],
        out_specs=vmem,
        scratch_shapes=[dma((7,)), dma((3,)), dma((4,))],
        compiler_params=pltpu.CompilerParams(collective_id=2, has_side_effects=True),
        name="gather_columns",
    )(mine)


def scatter_kernel(
    grad_ref,
    adj_ref,
    self_ref,
    term_ref,
    out_ref,
    weight_ref,
    cb,
    pbuf,
    zr,
    yr,
    yh,
    tr,
    swap_send,
    own_sem,
    part_recv,
    line_send,
    z_recv,
    y_recv,
    h_recv,
    term_send,
    term_recv,
):
    at = Place()
    b, r, nb, nr, nz = at.b, at.r, at.nb, at.nr, at.nz
    rows, wide = out_ref.shape
    half = rows // 2
    greet([((b + d) % nb, r) for d in range(1, nb)] + at.rep_peers())
    for d in range(1, nb):
        goal = (b + d) % nb
        remote(term_ref.at[goal], tr.at[b], term_send, term_recv, goal, r).start()

    tile = 256
    across_rows = (((0,), (0,)), ((), ()))
    for step in (2, 1, 3, 0):

        def tiles(n, carry, step=step):
            cols = pl.ds(pl.multiple_of(n * tile, tile), tile)
            out = lax.dot_general(
                adj_ref[step], grad_ref[:, cols], across_rows, preferred_element_type=F32
            )
            cb[step, :, :, cols] = out.astype(BF16).reshape(nr, rows, tile)
            return carry

        lax.fori_loop(0, wide // tile, tiles, 0)
        c = (b - r - nr * step + 2 * nb) % nb
        pltpu.make_async_copy(cb.at[step, r], pbuf.at[c], own_sem.at[step]).start()
        for d in (1, 7, 2, 6, 3, 5, 4):
            goal = (r + d) % nr
            remote(
                cb.at[step, goal], pbuf.at[c], swap_send, part_recv.at[c], b, goal
            ).start()
    for step in range(4):
        c = (b - r - nr * step + 2 * nb) % nb
        pltpu.make_async_copy(cb.at[step, r], pbuf.at[c], own_sem.at[step]).wait()

    def own(dyi, dz):
        c = at.block(DYS[dyi], dz)

        @pl.when((b - c + nb) % nr != r)
        def _():
            remote(pbuf.at[c], pbuf.at[c], swap_send, part_recv.at[c], b, r).wait_recv()

        return c

    reach = nz // 2
    for t in range(reach, 0, -1):
        for dyi in range(4):
            for wi, way in ((0, 1), (1, -1)):
                first = reach if (way == 1) == (dyi < 2) else reach - 1
                if t > first:
                    continue
                c = own(dyi, t * way)
                if t < first:
                    remote(
                        pbuf.at[c], zr.at[wi, dyi, t], line_send, z_recv.at[wi, dyi, t], b, r
                    ).wait_recv()
                    pbuf[c] = (pbuf[c].astype(F32) + zr[wi, dyi, t].astype(F32)).astype(BF16)
                remote(
                    pbuf.at[c],
                    zr.at[wi, dyi, t - 1],
                    line_send,
                    z_recv.at[wi, dyi, t - 1],
                    at.block(0, way),
                    r,
                ).start()

    def column(dyi):
        c = own(dyi, 0)
        for wi in range(2):
            remote(
                pbuf.at[c], zr.at[wi, dyi, 0], line_send, z_recv.at[wi, dyi, 0], b, r
            ).wait_recv()
        return c, pbuf[c].astype(F32) + zr[0, dyi, 0].astype(F32) + zr[1, dyi, 0].astype(F32)

    c, value = column(3)
    pbuf[c] = value.astype(BF16)
    for i, dy in ((0, 1), (1, -1)):
        part = pl.ds(i * half, half)
        remote(
            pbuf.at[c, part], yh.at[i], line_send, h_recv.at[i], at.block(dy, 0), r
        ).start()
    for i, (dyi, dy) in enumerate(((2, 1), (1, -1))):
        c, value = column(dyi)
        pbuf[c] = value.astype(BF16)
        remote(yh.at[i], yh.at[i], line_send, h_recv.at[i], b, r).wait_recv()
        part = pl.ds(i * half, half)
        pbuf[c, part] = (value[i * half : (i + 1) * half] + yh[i].astype(F32)).astype(BF16)
        remote(pbuf.at[c], yr.at[i], line_send, y_recv.at[i], at.block(dy, 0), r).start()
    c, value = column(0)
    value = value + self_ref[...]
    for i in range(2):
        remote(yr.at[i], yr.at[i], line_send, y_recv.at[i], b, r).wait_recv()
        value = value + yr[i].astype(F32)
    out_ref[...] = value.astype(BF16)

    some = tr.at[pl.ds(0, nb - 1)]
    remote(some, some, term_send, term_recv, b, at.sib).wait()
    tr[b] = term_ref[b]
    weight_ref[...] = jnp.sum(tr[...].astype(F32), axis=0)

    count = 4 * (nz - 1) + 3
    some = pbuf.at[pl.ds(0, count)]
    remote(some, some, line_send, term_recv, b, at.sib).wait_send()
    some = pbuf.at[pl.ds(0, 4 * (nr - 1))]
    remote(some, some, swap_send, term_recv, b, at.sib).wait_send()


def scatter_gradients(grad_agg, adj, self_rows, weight_term):
    rows, wide = self_rows.shape
    nb, nr = lax.axis_size("blk"), lax.axis_size("rep")
    thin, width = weight_term.shape
    terms = weight_term.reshape(nb, thin // nb, width)
    dma = pltpu.SemaphoreType.DMA
    vmem = pl.BlockSpec(memory_space=pltpu.VMEM)
    reach = nb // NY // 2
    return pl.pallas_call(
        scatter_kernel,
        out_shape=(
            jax.ShapeDtypeStruct((rows, wide), BF16),
            jax.ShapeDtypeStruct((thin // nb, width), F32),
        ),
        in_specs=[vmem] * 4,
        out_specs=(vmem, vmem),
        scratch_shapes=[
            pltpu.VMEM((nb // nr, nr, rows, wide), BF16),
            pltpu.VMEM((nb, rows, wide), BF16),
            pltpu.VMEM((2, 4, reach, rows, wide), BF16),
            pltpu.VMEM((2, rows, wide), BF16),
            pltpu.VMEM((2, rows // 2, wide), BF16),
            pltpu.VMEM(terms.shape, BF16),
            dma(()),
            dma((4,)),
            dma((nb,)),
            dma(()),
            dma((2, 4, reach)),
            dma((2,)),
            dma((2,)),
            dma(()),
            dma(()),
        ],
        compiler_params=pltpu.CompilerParams(
            collective_id=3, has_side_effects=True, vmem_limit_bytes=48 << 20
        ),
        name="scatter_gradients",
    )(grad_agg, adj, self_rows, terms)


def dense_blocks(tiles, counts, coords):
    steps, slots, tile, _ = tiles.shape
    slot_ids = jnp.arange(slots, dtype=jnp.int32)
    live = slot_ids[None, :] < counts[:, None]
    picked = []
    for i in range(2):
        row = []
        for j in range(2):
            chosen = live & (coords[..., 0] == i) & (coords[..., 1] == j)
            block = jnp.zeros((steps, tile, tile), BF16)
            for t in range(slots):
                block = jnp.where(chosen[:, t, None, None], tiles[:, t], block)
            row.append(block)
        picked.append(jnp.concatenate(row, axis=2))
    return jnp.concatenate(picked, axis=1)


def body(
    features,
    node_order,
    adj_tiles,
    counts,
    coords,
    w_self,
    w_neigh,
    norm_gain,
    norm_bias,
    mean_scale,
    cotangent,
):
    nb, nr = lax.axis_size("blk"), lax.axis_size("rep")
    rep = lax.axis_index("rep")
    rows_blk, wide = features.shape
    width = cotangent.shape[1]
    nodes = rows_blk * nb
    rows = rows_blk // nr
    adj = dense_blocks(adj_tiles[0, 0], counts.reshape(-1), coords[0, 0])

    ids = jnp.arange(rows_blk, dtype=jnp.int32)
    pick = (node_order[:, None] == ids[None, :]).astype(BF16)
    reordered = jnp.dot(pick, features, preferred_element_type=F32).astype(BF16)
    piece = lax.dynamic_slice_in_dim(reordered, rep * rows, rows, 0)
    aggregate = gather_features(piece, adj).reshape(rows_blk, wide)

    self_cols = lax.dynamic_slice_in_dim(w_self, rep * width, width, 1)
    neigh_cols = lax.dynamic_slice_in_dim(w_neigh, rep * width, width, 1)
    pre_norm = jnp.dot(reordered, self_cols, preferred_element_type=F32) + jnp.dot(
        aggregate, neigh_cols, preferred_element_type=F32
    )
    upstream = cotangent.astype(F32)
    near_mean = jnp.mean(pre_norm, axis=0)
    spread_off = pre_norm - near_mean
    local = jnp.stack(
        [
            near_mean,
            jnp.sum(spread_off * spread_off, axis=0),
            jnp.sum(upstream, axis=0),
            jnp.sum(upstream * spread_off, axis=0),
        ]
    )
    every = share_stats(jnp.concatenate([local, jnp.zeros_like(local)], axis=0))
    means, squares, cots, crosses = (every[:, i] for i in range(4))
    col_mean = jnp.sum(means, axis=0) / nb
    moved = means - mean_scale * col_mean
    spread = jnp.sum(squares + rows_blk * moved * moved, axis=0) / nodes
    cot_sum = jnp.sum(cots, axis=0)
    cot_cent = jnp.sum(crosses + cots * moved, axis=0)

    centered = pre_norm - mean_scale * col_mean
    col_scale = jnp.sqrt(spread + EPSILON)
    normed = (norm_gain * centered / col_scale + norm_bias).astype(BF16)
    grad_centered = norm_gain * upstream / col_scale - centered * (
        norm_gain * cot_cent / (nodes * col_scale**3)
    )
    grad_cent_total = (
        norm_gain * cot_sum / col_scale
        - (1.0 - mean_scale) * col_mean * norm_gain * cot_cent / col_scale**3
    )
    grad_pre = (grad_centered - mean_scale * grad_cent_total / nodes).astype(BF16)

    grad_full = gather_columns(grad_pre)
    by_cols = (((1,), (1,)), ((), ()))
    by_nodes = (((0,), (0,)), ((), ()))
    grad_agg = lax.dot_general(
        grad_full, w_neigh, by_cols, preferred_element_type=F32
    ).astype(BF16)
    own_rows = lax.dynamic_slice_in_dim(grad_full, rep * rows, rows, 0)
    self_rows = lax.dot_general(own_rows, w_self, by_cols, preferred_element_type=F32)
    weight_term = lax.dot_general(
        aggregate, grad_pre, by_nodes, preferred_element_type=F32
    ).astype(BF16)
    grad_feats, weight_sum = scatter_gradients(grad_agg, adj, self_rows, weight_term)
    grad_neigh = weight_sum / nodes
    grad_norm = jnp.stack([cot_cent / col_scale, cot_sum, -col_mean * grad_cent_total]) / nodes
    return (normed, grad_feats, grad_neigh, grad_norm)


def solution(mesh):
    in_specs = (
        P("blk", None),
        P("blk"),
        P("blk", "rep", None, None, None, None),
        P("blk", "rep", None),
        P("blk", "rep", None, None, None),
        P(),
        P(),
        P("rep"),
        P("rep"),
        P("rep"),
        P("blk", "rep"),
    )
    out_specs = (P("blk", "rep"), P(("blk", "rep"), None), P("blk", "rep"), P(None, "rep"))
    return jax.shard_map(body, mesh=mesh, in_specs=in_specs, out_specs=out_specs, check_vma=False)
```

```python
import jax
import jax.numpy as jnp
from jax import lax
from jax.experimental import pallas as pl
from jax.experimental.pallas import tpu as pltpu
from jax.sharding import PartitionSpec as P

EPSILON = 1e-05
MESH = pl.DeviceIdType.MESH
NY = 4
NX = 4
BF16 = jnp.bfloat16
F32 = jnp.float32


def remote(src, dst, send_sem, recv_sem, blk, rep):
    return pltpu.make_async_remote_copy(
        src_ref=src,
        dst_ref=dst,
        send_sem=send_sem,
        recv_sem=recv_sem,
        device_id=(blk, rep),
        device_id_type=MESH,
    )


def greet(peers):
    barrier = pltpu.get_barrier_semaphore()
    for blk, rep in peers:
        pl.semaphore_signal(barrier, inc=1, device_id=(blk, rep), device_id_type=MESH)
    pl.semaphore_wait(barrier, len(peers))


class Place:
    def __init__(self):
        self.b = lax.axis_index("blk")
        self.r = lax.axis_index("rep")
        self.nb = lax.axis_size("blk")
        self.nr = lax.axis_size("rep")
        self.nz = self.nb // NY
        self.y = self.b % NY
        self.z = self.b // NY
        self.x = self.r // 2
        self.k = self.r % 2
        self.sib = self.x * 2 + (1 - self.k)

    def block(self, dy, dz):
        return ((self.z + dz + self.nz) % self.nz) * NY + (self.y + dy + NY) % NY

    def across(self, dx):
        return ((self.x + dx) % NX) * 2 + self.k

    def torus_peers(self):
        steps = ((1, 0), (-1, 0), (0, 1), (0, -1))
        return [(self.block(dy, dz), self.r) for dy, dz in steps]

    def rep_peers(self):
        return [(self.b, (self.r + d) % self.nr) for d in range(1, self.nr)]

    def line_peers(self):
        return [(self.b, self.across(d)) for d in range(1, NX)] + [(self.b, self.sib)]


DYS = (0, -1, 1, 2)
ROW_TILE = 128
COL_TILE = 256
BY_FIRST = (((0,), (0,)), ((), ()))
BY_LAST = (((1,), (1,)), ((), ()))


def layer_kernel(
    feat_hbm,
    order_ref,
    tiles_hbm,
    counts_ref,
    coords_ref,
    self_hbm,
    neigh_hbm,
    gain_ref,
    bias_ref,
    scale_ref,
    cot_ref,
    normed_ref,
    out_ref,
    weight_ref,
    norm_ref,
    feat,
    tiles,
    w_self,
    w_neigh,
    load_sem,
    reordered,
    adj,
    self_pre,
    g,
    o,
    acc,
    pb,
    rb1,
    qb,
    rb2,
    agg,
    prod,
    prod_in,
    pre,
    stat,
    stats,
    grad_pre,
    grad_all,
    grad_agg,
    self_rows,
    term,
    term_in,
    cb,
    pbuf,
    zr,
    yr,
    yh,
    piece_recv,
    half_recv,
    line_send,
    swap_send,
    swap_recv,
    own_sem,
    red_send,
    red_recv1,
    red_recv2,
    prod_send,
    prod_recv,
    agg_send,
    agg_recv,
    agg_sib,
    stat_send,
    stat_recv,
    col_send,
    col_recv,
    col_sib,
    term_send,
    term_recv,
    back_own,
    back_send,
    part_recv,
    back_line,
    z_recv,
    y_recv,
    h_recv,
):
    at = Place()
    b, r, nb, nr, nz = at.b, at.r, at.nb, at.nr, at.nz
    x, k, sib = at.x, at.k, at.sib
    rows, wide = out_ref.shape
    half = rows // 2
    rows_blk = rows * nr
    width = cot_ref.shape[1]
    nodes = rows_blk * nb
    reach = nz // 2
    sides = rows_blk // tiles.shape[-1]
    side = tiles.shape[-1]
    slots = tiles.shape[1]

    loads = [
        pltpu.make_async_copy(src, dst, load_sem.at[i])
        for i, (src, dst) in enumerate(
            ((feat_hbm, feat), (tiles_hbm, tiles), (self_hbm, w_self), (neigh_hbm, w_neigh))
        )
    ]
    for load in loads:
        load.start()

    def reorder(low):
        ids = lax.broadcasted_iota(jnp.int32, (rows_blk, ROW_TILE), 0)
        want = order_ref[:, pl.ds(pl.multiple_of(low, ROW_TILE), ROW_TILE)]
        pick = jnp.where(ids == want, 1.0, 0.0).astype(BF16)
        return lax.dot_general(pick, feat[...], BY_FIRST, preferred_element_type=F32).astype(BF16)

    greet([((b + d) % nb, r) for d in range(1, nb)] + at.rep_peers())
    loads[0].wait()
    reordered[x] = reorder(x * ROW_TILE)
    g[b] = reordered[x, pl.ds(pl.multiple_of(k * rows, rows), rows), :]

    def to_line(dyi, dz, dz_step):
        c = at.block(DYS[dyi], dz)
        target = (dz - dz_step) % nz
        remote(
            g.at[c], g.at[c], line_send, piece_recv.at[dyi, target], at.block(0, dz_step), r
        ).start()

    def hand_out(dyi, dz):
        c = at.block(DYS[dyi], dz)
        diff = (b - c + nb) % nb
        goal = diff % nr
        step = diff // nr

        @pl.when(goal != r)
        def _():
            remote(
                g.at[c], o.at[step, r], swap_send, swap_recv.at[step], b, goal
            ).start()

        @pl.when(goal == r)
        def _():
            pltpu.make_async_copy(g.at[c], o.at[step, r], own_sem.at[step]).start()

    def arrive(dyi, dz):
        c = at.block(DYS[dyi], dz)
        remote(
            g.at[c], g.at[c], line_send, piece_recv.at[dyi, dz % nz], b, r
        ).wait_recv()

    def fill_block(step):
        def run():
            if step == 0:
                loads[1].wait()
            for i in range(sides):
                for j in range(sides):
                    block = jnp.zeros((side, side), F32)
                    for t in range(slots):
                        live = (
                            (t < counts_ref[step])
                            & (coords_ref[step, t, 0] == i)
                            & (coords_ref[step, t, 1] == j)
                        )
                        chosen = jnp.where(live, 1.0, 0.0)
                        block = block + chosen * tiles[step, t].astype(F32)
                    adj[step, i * side : (i + 1) * side, j * side : (j + 1) * side] = block.astype(BF16)

        return run

    def fill_rows(d):
        def run():
            n = (x + d) % NX
            if d:
                reordered[n] = reorder(n * ROW_TILE)
            if d == 0:
                loads[2].wait()
            cols = pl.ds(pl.multiple_of(r * width, width), width)
            self_pre[n] = jnp.dot(reordered[n], w_self[:, cols], preferred_element_type=F32)

        return run

    work = [fill_block(step) for step in range(nb // nr)] + [fill_rows(d) for d in range(NX)]

    for dyi, dy in ((2, -1), (1, 1)):
        remote(
            g.at[b], g.at[b], line_send, piece_recv.at[dyi, 0], at.block(dy, 0), r
        ).start()
    to_line(0, 0, 1)
    to_line(0, 0, -1)
    hand_out(0, 0)
    for dyi, onward, low in ((1, 1, 0), (2, -1, half)):
        arrive(dyi, 0)
        c = at.block(DYS[dyi], 0)
        part = pl.ds(low, half)
        remote(
            g.at[c, part], g.at[c, part], line_send, half_recv.at[dyi - 1], at.block(onward, 0), r
        ).start()
        to_line(dyi, 0, 1)
        to_line(dyi, 0, -1)
        hand_out(dyi, 0)
    far = at.block(2, 0)
    for i, low in ((0, 0), (1, half)):
        part = pl.ds(low, half)
        remote(
            g.at[far, part], g.at[far, part], line_send, half_recv.at[i], b, r
        ).wait_recv()
    to_line(3, 0, 1)
    to_line(3, 0, -1)
    hand_out(3, 0)
    for t in range(1, reach):
        for dyi in range(4):
            for way in (1, -1):
                dz = -t * way
                arrive(dyi, dz)
                if t < reach - 1 or (way == 1) == (dyi < 2):
                    to_line(dyi, dz, way)
                hand_out(dyi, dz)
            if work:
                work.pop(0)()
    for dyi in (0, 2, 1, 3):
        arrive(dyi, reach)
        hand_out(dyi, reach)

    for i, step in enumerate((0, 1, 3, 2)):
        pltpu.make_async_copy(o.at[step, 0], o.at[step, 0], own_sem.at[step]).wait()
        some = o.at[step, pl.ds(0, nr - 1)]
        remote(some, some, swap_send, swap_recv.at[step], b, r).wait_recv()

        def part_tile(n, carry, step=step, i=i):
            cols = pl.ds(pl.multiple_of(n * COL_TILE, COL_TILE), COL_TILE)
            source = o[step, :, :, cols].reshape(rows_blk, COL_TILE)
            out = jnp.dot(adj[step], source, preferred_element_type=F32)
            acc[:, cols] = out if i == 0 else acc[:, cols] + out
            return carry

        lax.fori_loop(0, wide // COL_TILE, part_tile, 0)

    def chunk(m):
        return acc[pl.ds(pl.multiple_of(m * rows, rows), rows), :]

    for m in range(NX):
        pb[m] = chunk((1 - k) * NX + m).astype(BF16)
    swap_halves = remote(pb, rb1, red_send.at[0], red_recv1, b, sib)
    swap_halves.start()
    loads[3].wait()
    swap_halves.wait_recv()

    def reduced(d):
        return remote(
            qb.at[d - 1], rb2.at[d - 1], red_send.at[d], red_recv2.at[d - 1], b, at.across(d)
        )

    for d in (2, 1, 3):
        goal = (x + d) % NX
        qb[d - 1] = (chunk(k * NX + goal) + rb1[goal].astype(F32)).astype(BF16)
        reduced(d).start()
    home = k * NX + x
    total = chunk(home) + rb1[x].astype(F32)
    for d in (1, 3, 2):
        reduced(d).wait_recv()
        total = total + rb2[d - 1].astype(F32)
    agg[home] = total.astype(BF16)

    for n in range(wide // COL_TILE):
        cols = slice(n * COL_TILE, (n + 1) * COL_TILE)
        out = jnp.dot(agg[home], w_neigh[:, cols], preferred_element_type=F32)
        for j in range(COL_TILE // width):
            prod[n * (COL_TILE // width) + j] = out[:, j * width : (j + 1) * width]
    for d in (4, 5, 2, 3, 6, 7, 1):
        goal = (r + d) % nr
        remote(prod.at[goal], prod_in.at[home], prod_send, prod_recv, b, goal).start()
    prod_in[home] = prod[r]

    def agg_line(d):
        return remote(
            agg.at[home], agg.at[home], agg_send.at[d - 1], agg_recv.at[d - 1], b, at.across(d)
        )

    for d in (2, 1, 3):
        agg_line(d).start()
    remote(agg.at[home], agg.at[home], agg_send.at[3], agg_sib.at[0], b, sib).start()
    some = prod_in.at[pl.ds(0, nr - 1)]
    remote(some, some, prod_send, prod_recv, b, sib).wait_recv()

    pre[...] = self_pre[...].reshape(rows_blk, width) + prod_in[...].reshape(rows_blk, width)
    upstream = cot_ref[...].astype(F32)
    near_mean = jnp.sum(pre[...], axis=0, keepdims=True) / rows_blk
    off = pre[...] - near_mean
    stat[0:1, :] = near_mean
    stat[1:2, :] = jnp.sum(off * off, axis=0, keepdims=True)
    stat[2:3, :] = jnp.sum(upstream, axis=0, keepdims=True)
    stat[3:4, :] = jnp.sum(upstream * off, axis=0, keepdims=True)
    stat[4:8, :] = jnp.zeros((4, width), F32)
    for d in range(1, nb):
        remote(stat, stats.at[b], stat_send, stat_recv, (b + d) % nb, r).start()
    stats[b] = stat[...]
    some = stats.at[pl.ds(0, nb - 1)]
    remote(some, some, stat_send, stat_recv, b, sib).wait_recv()

    gain, mean_scale = gain_ref[...], scale_ref[...]
    means, cots = stats[:, 0, :], stats[:, 2, :]
    col_mean = jnp.sum(means, axis=0, keepdims=True) / nb
    moved = means - mean_scale * col_mean
    spread = (
        jnp.sum(stats[:, 1, :] + rows_blk * moved * moved, axis=0, keepdims=True) / nodes
    )
    cot_sum = jnp.sum(cots, axis=0, keepdims=True)
    cot_cent = jnp.sum(stats[:, 3, :] + cots * moved, axis=0, keepdims=True)
    col_scale = jnp.sqrt(spread + EPSILON)
    cube = col_scale * col_scale * col_scale
    sharp = gain / col_scale
    weight = gain * cot_cent / (nodes * cube)
    grad_cent_total = sharp * cot_sum - (1.0 - mean_scale) * col_mean * gain * cot_cent / cube
    centered = pre[...] - mean_scale * col_mean
    grad_pre[...] = (
        sharp * upstream - centered * weight - mean_scale * grad_cent_total / nodes
    ).astype(BF16)

    def columns(rep):
        return grad_all.at[:, pl.ds(pl.multiple_of(rep * width, width), width)]

    for d in (2, 1, 3):
        remote(
            grad_pre, columns(r), col_send.at[d - 1], col_recv.at[d - 1], b, at.across(d)
        ).start()
    remote(grad_pre, columns(r), col_send.at[3], col_sib.at[0], b, sib).start()
    grad_all[:, pl.ds(pl.multiple_of(r * width, width), width)] = grad_pre[...]
    normed_ref[...] = (sharp * centered + bias_ref[...]).astype(BF16)
    norm_ref[0:1, :] = cot_cent / col_scale / nodes
    norm_ref[1:2, :] = cot_sum / nodes
    norm_ref[2:3, :] = -col_mean * grad_cent_total / nodes
    for d in (1, 3, 2):
        came = k * NX + (x - d + NX) % NX
        remote(
            agg.at[came], agg.at[came], agg_send.at[d - 1], agg_recv.at[d - 1], b, sib
        ).wait_recv()
        remote(agg.at[came], agg.at[came], agg_send.at[3 + d], agg_sib.at[d], b, sib).start()
    for d in (1, 3, 2):
        came = columns(at.across(NX - d))
        remote(came, came, col_send.at[d - 1], col_recv.at[d - 1], b, sib).wait_recv()
        remote(came, came, col_send.at[3 + d], col_sib.at[d], b, sib).start()
    for d in range(4):
        came = columns(((x - d + NX) % NX) * 2 + (1 - k))
        remote(came, came, col_send.at[3], col_sib.at[d], b, sib).wait_recv()

    def agg_tile(n, carry):
        low = pl.ds(pl.multiple_of(n * COL_TILE, COL_TILE), COL_TILE)
        out = lax.dot_general(
            grad_all[...], w_neigh[low, :], BY_LAST, preferred_element_type=F32
        )
        grad_agg[:, low] = out.astype(BF16)
        return carry

    lax.fori_loop(0, wide // COL_TILE, agg_tile, 0)

    for step in (2, 1, 3, 0):

        def back_tile(n, carry, step=step):
            cols = pl.ds(pl.multiple_of(n * COL_TILE, COL_TILE), COL_TILE)
            out = lax.dot_general(
                adj[step], grad_agg[:, cols], BY_FIRST, preferred_element_type=F32
            )
            cb[step, :, :, cols] = out.astype(BF16).reshape(nr, rows, COL_TILE)
            return carry

        lax.fori_loop(0, wide // COL_TILE, back_tile, 0)
        c = (b - r - nr * step + 2 * nb) % nb
        pltpu.make_async_copy(cb.at[step, r], pbuf.at[c], back_own.at[step]).start()
        for d in (1, 7, 2, 6, 3, 5, 4):
            goal = (r + d) % nr
            remote(
                cb.at[step, goal], pbuf.at[c], back_send, part_recv.at[c], b, goal
            ).start()
    for d in range(4):
        came = (1 - k) * NX + (x - d + NX) % NX
        remote(agg.at[came], agg.at[came], agg_send.at[3], agg_sib.at[d], b, sib).wait_recv()
    thin = weight_ref.shape[0]
    for n in range(wide // COL_TILE):
        cols = slice(n * COL_TILE, (n + 1) * COL_TILE)
        source = agg[:, :, cols].reshape(rows_blk, COL_TILE)
        out = lax.dot_general(source, grad_pre[...], BY_FIRST, preferred_element_type=F32)
        each = COL_TILE // thin
        term[n * each : (n + 1) * each] = out.astype(BF16).reshape(each, thin, width)
    for d in range(1, nb):
        goal = (b + d) % nb
        remote(term.at[goal], term_in.at[b], term_send, term_recv, goal, r).start()
    term_in[b] = term[b]
    own_rows = pl.ds(pl.multiple_of(r * rows, rows), rows)
    self_rows[...] = lax.dot_general(
        grad_all[own_rows, :], w_self[...], BY_LAST, preferred_element_type=F32
    )
    for step in range(4):
        c = (b - r - nr * step + 2 * nb) % nb
        pltpu.make_async_copy(cb.at[step, r], pbuf.at[c], back_own.at[step]).wait()

    def own(dyi, dz):
        c = at.block(DYS[dyi], dz)

        @pl.when((b - c + nb) % nr != r)
        def _():
            remote(pbuf.at[c], pbuf.at[c], back_send, part_recv.at[c], b, r).wait_recv()

        return c

    for t in range(reach, 0, -1):
        for dyi in range(4):
            for wi, way in ((0, 1), (1, -1)):
                first = reach if (way == 1) == (dyi < 2) else reach - 1
                if t > first:
                    continue
                c = own(dyi, t * way)
                if t < first:
                    remote(
                        pbuf.at[c], zr.at[wi, dyi, t], back_line, z_recv.at[wi, dyi, t], b, r
                    ).wait_recv()
                    pbuf[c] = (pbuf[c].astype(F32) + zr[wi, dyi, t].astype(F32)).astype(BF16)
                remote(
                    pbuf.at[c],
                    zr.at[wi, dyi, t - 1],
                    back_line,
                    z_recv.at[wi, dyi, t - 1],
                    at.block(0, way),
                    r,
                ).start()

    def column(dyi):
        c = own(dyi, 0)
        for wi in range(2):
            remote(
                pbuf.at[c], zr.at[wi, dyi, 0], back_line, z_recv.at[wi, dyi, 0], b, r
            ).wait_recv()
        return c, pbuf[c].astype(F32) + zr[0, dyi, 0].astype(F32) + zr[1, dyi, 0].astype(F32)

    c, value = column(3)
    pbuf[c] = value.astype(BF16)
    for i, dy in ((0, 1), (1, -1)):
        part = pl.ds(i * half, half)
        remote(
            pbuf.at[c, part], yh.at[i], back_line, h_recv.at[i], at.block(dy, 0), r
        ).start()
    for i, (dyi, dy) in enumerate(((2, 1), (1, -1))):
        c, value = column(dyi)
        pbuf[c] = value.astype(BF16)
        remote(yh.at[i], yh.at[i], back_line, h_recv.at[i], b, r).wait_recv()
        part = pl.ds(i * half, half)
        pbuf[c, part] = (value[i * half : (i + 1) * half] + yh[i].astype(F32)).astype(BF16)
        remote(pbuf.at[c], yr.at[i], back_line, y_recv.at[i], at.block(dy, 0), r).start()
    c, value = column(0)
    value = value + self_rows[...]
    for i in range(2):
        remote(yr.at[i], yr.at[i], back_line, y_recv.at[i], b, r).wait_recv()
        value = value + yr[i].astype(F32)
    out_ref[...] = value.astype(BF16)

    some = term_in.at[pl.ds(0, nb - 1)]
    remote(some, some, term_send, term_recv, b, sib).wait()
    weight_ref[...] = jnp.sum(term_in[...].astype(F32), axis=0) / nodes

    def sent(some, sem):
        remote(some, some, sem, term_recv, b, sib).wait_send()

    sent(g.at[pl.ds(0, 3 + 4 * (nz - 1))], line_send)
    sent(g.at[pl.ds(0, 4 * (nr - 1))], swap_send)
    sent(pbuf.at[pl.ds(0, 3 + 4 * (nz - 1))], back_line)
    sent(pbuf.at[pl.ds(0, 4 * (nr - 1))], back_send)
    sent(pb, red_send.at[0])
    for d in range(1, NX):
        sent(qb.at[d - 1], red_send.at[d])
    for i in range(7):
        sent(agg.at[0], agg_send.at[i])
        sent(grad_pre, col_send.at[i])
    sent(prod_in.at[pl.ds(0, nr - 1)], prod_send)
    sent(stats.at[pl.ds(0, nb - 1)], stat_send)


def body(
    features,
    node_order,
    adj_tiles,
    counts,
    coords,
    w_self,
    w_neigh,
    norm_gain,
    norm_bias,
    mean_scale,
    cotangent,
):
    nb, nr = lax.axis_size("blk"), lax.axis_size("rep")
    rows_blk, wide = features.shape
    width = cotangent.shape[1]
    rows = rows_blk // nr
    thin = wide // nb
    steps = nb // nr
    reach = nb // NY // 2
    tiles = adj_tiles[0, 0]
    dma = pltpu.SemaphoreType.DMA
    vmem = pl.BlockSpec(memory_space=pltpu.VMEM)
    smem = pl.BlockSpec(memory_space=pltpu.SMEM)
    hbm = pl.BlockSpec(memory_space=pl.ANY)

    def room(*shape, dtype=BF16):
        return pltpu.VMEM(shape, dtype)

    return tuple(
        pl.pallas_call(
            layer_kernel,
            out_shape=(
                jax.ShapeDtypeStruct((rows_blk, width), BF16),
                jax.ShapeDtypeStruct((rows, wide), BF16),
                jax.ShapeDtypeStruct((thin, width), F32),
                jax.ShapeDtypeStruct((3, width), F32),
            ),
            in_specs=[hbm, vmem, hbm, smem, smem, hbm, hbm, vmem, vmem, vmem, vmem],
            out_specs=(vmem,) * 4,
            scratch_shapes=[
                room(rows_blk, wide),
                room(*tiles.shape),
                room(wide, wide),
                room(wide, wide),
                dma((4,)),
                room(NX, ROW_TILE, wide),
                room(steps, rows_blk, rows_blk),
                room(NX, ROW_TILE, width, dtype=F32),
                room(nb, rows, wide),
                room(steps, nr, rows, wide),
                room(rows_blk, wide, dtype=F32),
                room(NX, rows, wide),
                room(NX, rows, wide),
                room(NX - 1, rows, wide),
                room(NX - 1, rows, wide),
                room(nr, rows, wide),
                room(nr, rows, width, dtype=F32),
                room(nr, rows, width, dtype=F32),
                room(rows_blk, width, dtype=F32),
                room(8, width, dtype=F32),
                room(nb, 8, width, dtype=F32),
                room(rows_blk, width),
                room(rows_blk, wide),
                room(rows_blk, wide),
                room(rows, wide, dtype=F32),
                room(nb, thin, width),
                room(nb, thin, width),
                room(steps, nr, rows, wide),
                room(nb, rows, wide),
                room(2, 4, reach, rows, wide),
                room(2, rows, wide),
                room(2, rows // 2, wide),
                dma((4, nb // NY)),
                dma((2,)),
                dma(()),
                dma(()),
                dma((steps,)),
                dma((steps,)),
                dma((4,)),
                dma(()),
                dma((3,)),
                dma(()),
                dma(()),
                dma((7,)),
                dma((3,)),
                dma((4,)),
                dma(()),
                dma(()),
                dma((7,)),
                dma((3,)),
                dma((4,)),
                dma(()),
                dma(()),
                dma((steps,)),
                dma(()),
                dma((nb,)),
                dma(()),
                dma((2, 4, reach)),
                dma((2,)),
                dma((2,)),
            ],
            compiler_params=pltpu.CompilerParams(
                collective_id=0, has_side_effects=True, vmem_limit_bytes=56 << 20
            ),
            name="layer",
        )(
            features,
            node_order.reshape(1, rows_blk),
            tiles,
            counts.reshape(steps),
            coords[0, 0],
            w_self,
            w_neigh,
            norm_gain.reshape(1, width),
            norm_bias.reshape(1, width),
            mean_scale.reshape(1, width),
            cotangent,
        )
    )


def solution(mesh):
    in_specs = (
        P("blk", None),
        P("blk"),
        P("blk", "rep", None, None, None, None),
        P("blk", "rep", None),
        P("blk", "rep", None, None, None),
        P(),
        P(),
        P("rep"),
        P("rep"),
        P("rep"),
        P("blk", "rep"),
    )
    out_specs = (P("blk", "rep"), P(("blk", "rep"), None), P("blk", "rep"), P(None, "rep"))
    return jax.shard_map(body, mesh=mesh, in_specs=in_specs, out_specs=out_specs, check_vma=False)
```

```python
import jax
import jax.numpy as jnp
from jax import lax
from jax.experimental import pallas as pl
from jax.experimental.pallas import tpu as pltpu
from jax.sharding import PartitionSpec as P

EPSILON = 1e-05
MESH = pl.DeviceIdType.MESH
NY = 4
NX = 4
BF16 = jnp.bfloat16
F32 = jnp.float32


def remote(src, dst, send_sem, recv_sem, blk, rep):
    return pltpu.make_async_remote_copy(
        src_ref=src,
        dst_ref=dst,
        send_sem=send_sem,
        recv_sem=recv_sem,
        device_id=(blk, rep),
        device_id_type=MESH,
    )


def greet(peers):
    barrier = pltpu.get_barrier_semaphore()
    for blk, rep in peers:
        pl.semaphore_signal(barrier, inc=1, device_id=(blk, rep), device_id_type=MESH)
    pl.semaphore_wait(barrier, len(peers))


class Place:
    def __init__(self):
        self.b = lax.axis_index("blk")
        self.r = lax.axis_index("rep")
        self.nb = lax.axis_size("blk")
        self.nr = lax.axis_size("rep")
        self.nz = self.nb // NY
        self.y = self.b % NY
        self.z = self.b // NY
        self.x = self.r // 2
        self.k = self.r % 2
        self.sib = self.x * 2 + (1 - self.k)

    def block(self, dy, dz):
        return ((self.z + dz + self.nz) % self.nz) * NY + (self.y + dy + NY) % NY

    def across(self, dx):
        return ((self.x + dx) % NX) * 2 + self.k

    def torus_peers(self):
        steps = ((1, 0), (-1, 0), (0, 1), (0, -1))
        return [(self.block(dy, dz), self.r) for dy, dz in steps]

    def rep_peers(self):
        return [(self.b, (self.r + d) % self.nr) for d in range(1, self.nr)]

    def line_peers(self):
        return [(self.b, self.across(d)) for d in range(1, NX)] + [(self.b, self.sib)]


ROW_TILE = 128
COL_TILE = 256
BY_FIRST = (((0,), (0,)), ((), ()))
BY_LAST = (((1,), (1,)), ((), ()))


def layer_kernel(
    feat_hbm,
    order_ref,
    tiles_hbm,
    counts_ref,
    coords_ref,
    self_hbm,
    neigh_hbm,
    gain_ref,
    bias_ref,
    scale_ref,
    cot_ref,
    normed_ref,
    out_ref,
    weight_ref,
    norm_ref,
    feat,
    tiles,
    w_self,
    w_neigh,
    load_sem,
    reordered,
    adj,
    self_pre,
    g,
    o,
    acc,
    pb,
    rb1,
    qb,
    rb2,
    agg,
    prod,
    prod_in,
    pre,
    stat,
    stats,
    grad_pre,
    grad_all,
    grad_agg,
    self_rows,
    term,
    term_in,
    cb,
    pbuf,
    zr,
    yr,
    yh,
    qin,
    qside,
    owed,
    lent,
    line_recv,
    side_recv,
    plane_send,
    plane_recv,
    line_send,
    swap_send,
    swap_recv,
    own_sem,
    red_send,
    red_recv1,
    red_recv2,
    prod_send,
    prod_recv,
    agg_send,
    agg_recv,
    agg_sib,
    stat_send,
    stat_recv,
    col_send,
    col_recv,
    col_sib,
    term_send,
    term_recv,
    back_own,
    back_send,
    part_recv,
    back_line,
    z_recv,
    y_recv,
    h_recv,
    chain_send,
    chain_recv,
    lent_send,
    lent_recv,
):
    at = Place()
    b, r, nb, nr, nz = at.b, at.r, at.nb, at.nr, at.nz
    x, k, sib = at.x, at.k, at.sib
    rows, wide = out_ref.shape
    half = rows // 2
    rows_blk = rows * nr
    width = cot_ref.shape[1]
    nodes = rows_blk * nb
    reach = nz // 2
    sides = rows_blk // tiles.shape[-1]
    side = tiles.shape[-1]
    slots = tiles.shape[1]
    steps = nb // nr

    loads = [
        pltpu.make_async_copy(src, dst, load_sem.at[i])
        for i, (src, dst) in enumerate(
            ((feat_hbm, feat), (tiles_hbm, tiles), (self_hbm, w_self), (neigh_hbm, w_neigh))
        )
    ]
    for load in loads:
        load.start()

    def reorder(low):
        ids = lax.broadcasted_iota(jnp.int32, (rows_blk, ROW_TILE), 0)
        want = order_ref[:, pl.ds(pl.multiple_of(low, ROW_TILE), ROW_TILE)]
        pick = jnp.where(ids == want, 1.0, 0.0).astype(BF16)
        return lax.dot_general(pick, feat[...], BY_FIRST, preferred_element_type=F32).astype(BF16)

    greet([((b + d) % nb, r) for d in range(1, nb)] + at.rep_peers())
    loads[0].wait()
    reordered[x] = reorder(x * ROW_TILE)
    g[b] = reordered[x, pl.ds(pl.multiple_of(k * rows, rows), rows), :]

    opposite = (x + 2) % NX
    far_blk = nb // steps

    def pass_on(c, sem, blk, low=0, count=rows):
        part = pl.ds(low, count)
        return remote(g.at[c, part], g.at[c, part], line_send, sem, blk, r)

    def hand_out(dy, dz):
        c = at.block(dy, dz)
        diff = (b - c + nb) % nb
        goal = diff % nr
        step = diff // nr
        slot = o.at[step, x, pl.ds(pl.multiple_of(k * rows, rows), rows)]

        @pl.when((goal != r) & (goal // 2 != opposite))
        def _():
            remote(g.at[c], slot, swap_send, swap_recv.at[step], b, goal).start()

        @pl.when(goal == r)
        def _():
            pltpu.make_async_copy(g.at[c], slot, own_sem.at[step]).start()

    def fill_block(step):
        def run():
            if step == 0:
                loads[1].wait()
            for i in range(sides):
                for j in range(sides):
                    block = jnp.zeros((side, side), F32)
                    for t in range(slots):
                        live = (
                            (t < counts_ref[step])
                            & (coords_ref[step, t, 0] == i)
                            & (coords_ref[step, t, 1] == j)
                        )
                        chosen = jnp.where(live, 1.0, 0.0)
                        block = block + chosen * tiles[step, t].astype(F32)
                    adj[step, i * side : (i + 1) * side, j * side : (j + 1) * side] = block.astype(BF16)

        return run

    def fill_rows(d):
        def run():
            n = (x + d) % NX
            if d % 2:
                reordered[n] = reorder(n * ROW_TILE)
            if d == 0:
                loads[2].wait()
            cols = pl.ds(pl.multiple_of(r * width, width), width)
            self_pre[n] = jnp.dot(reordered[n], w_self[:, cols], preferred_element_type=F32)

        return run

    work = [fill_block(step) for step in range(steps)] + [fill_rows(d) for d in range(NX)]

    def slab(step, low=0, count=ROW_TILE):
        return o.at[step, opposite, pl.ds(low, count)]

    def relay(step_from, step_to, sem, blk, low=0, count=ROW_TILE):
        return remote(
            slab(step_from, low, count), slab(step_to, low, count), plane_send.at[0], plane_recv.at[sem], blk, r
        )

    def shift_out():
        return remote(
            reordered.at[opposite], slab(0), plane_send.at[1], plane_recv.at[0], (b + r) % nb, r
        )

    up, down = (b + far_blk) % nb, (b - far_blk + nb) % nb

    def plane_start():
        @pl.when(r != 0)
        def _():
            shift_out().start()

        @pl.when(r == 0)
        def _():
            o[0, opposite] = reordered[opposite]

    def plane_spread():
        @pl.when(r != 0)
        def _():
            shift_out().wait_recv()

        relay(0, 1, 1, up).start()
        relay(0, 3, 3, down).start()

    def plane_far():
        relay(0, 1, 1, up).wait_recv()
        relay(1, 2, 2, up, 0, rows).start()
        relay(0, 3, 3, down).wait_recv()
        relay(3, 2, 4, down, rows, rows).start()

    def plane_end():
        relay(1, 2, 2, up, 0, rows).wait_recv()
        relay(3, 2, 4, down, rows, rows).wait_recv()

    ORDER = [0] + [dz for t in range(1, reach) for dz in (-t, t)] + [reach]

    def column_step(i):
        dz = ORDER[i]
        c = at.block(0, dz)
        if dz == reach:
            for w in range(2):
                pass_on(c, line_recv.at[reach + w], b, w * half, half).wait_recv()
        elif dz:
            pass_on(c, line_recv.at[dz % nz + (dz < 0)], b).wait_recv()
        for w, way in ((0, 1), (1, -1)):
            if dz == 0 or (dz * way < 0 and abs(dz) < reach - 1):
                n = (dz - way) % nz
                pass_on(c, line_recv.at[n + (n > reach)], at.block(0, way)).start()
            elif dz * way == 1 - reach:
                pass_on(c, line_recv.at[reach + w], at.block(0, way), w * half, half).start()
        for w, way in ((0, 1), (1, -1)):
            pass_on(c, side_recv.at[w, i], at.block(way, 0)).start()
        hand_out(0, dz)

    def side_step(i):
        dz = ORDER[i]
        for w, way in ((0, 1), (1, -1)):
            c = at.block(-way, dz)
            pass_on(c, side_recv.at[w, i], b).wait_recv()
            pass_on(c, side_recv.at[2 + w, i], at.block(way, 0), w * half, half).start()
            hand_out(-way, dz)

    def far_step(i):
        dz = ORDER[i]
        c = at.block(2, dz)
        for w in range(2):
            pass_on(c, side_recv.at[2 + w, i], b, w * half, half).wait_recv()
        hand_out(2, dz)

    lag = 3
    for i in range(nz + lag + 1):
        if i < nz:
            column_step(i)
        if i == 0:
            reordered[opposite] = reorder(opposite * ROW_TILE)
            plane_start()
        if lag <= i < nz + lag:
            side_step(i - lag)
        if lag < i:
            far_step(i - lag - 1)
        if i == 3:
            plane_spread()
        if i == 7:
            plane_far()
        if i >= 2:
            if work:
                work.pop(0)()
    plane_end()

    for i, step in enumerate((0, 1, 3, 2)):
        some = o.at[step, 0, pl.ds(0, rows)]
        pltpu.make_async_copy(some, some, own_sem.at[step]).wait()
        some = g.at[pl.ds(0, nr - 3)]
        remote(some, some, swap_send, swap_recv.at[step], b, r).wait_recv()

        def part_tile(n, carry, step=step, i=i):
            cols = pl.ds(pl.multiple_of(n * COL_TILE, COL_TILE), COL_TILE)
            source = o[step, :, :, cols].reshape(rows_blk, COL_TILE)
            out = jnp.dot(adj[step], source, preferred_element_type=F32)
            acc[:, cols] = out if i == 0 else acc[:, cols] + out
            return carry

        lax.fori_loop(0, wide // COL_TILE, part_tile, 0)

    def chunk(m):
        return acc[pl.ds(pl.multiple_of(m * rows, rows), rows), :]

    for m in range(NX):
        pb[m] = chunk((1 - k) * NX + m).astype(BF16)
    swap_halves = remote(pb, rb1, red_send.at[0], red_recv1, b, sib)
    swap_halves.start()
    loads[3].wait()
    swap_halves.wait_recv()

    def reduced(d):
        return remote(
            qb.at[d - 1], rb2.at[d - 1], red_send.at[d], red_recv2.at[d - 1], b, at.across(d)
        )

    for d in (2, 1, 3):
        goal = (x + d) % NX
        qb[d - 1] = (chunk(k * NX + goal) + rb1[goal].astype(F32)).astype(BF16)
        reduced(d).start()
    home = k * NX + x
    total = chunk(home) + rb1[x].astype(F32)
    for d in (1, 3, 2):
        reduced(d).wait_recv()
        total = total + rb2[d - 1].astype(F32)
    agg[home] = total.astype(BF16)

    for n in range(wide // COL_TILE):
        cols = slice(n * COL_TILE, (n + 1) * COL_TILE)
        out = jnp.dot(agg[home], w_neigh[:, cols], preferred_element_type=F32)
        for j in range(COL_TILE // width):
            prod[n * (COL_TILE // width) + j] = out[:, j * width : (j + 1) * width]
    for d in (4, 5, 2, 3, 6, 7, 1):
        goal = (r + d) % nr
        remote(prod.at[goal], prod_in.at[home], prod_send, prod_recv, b, goal).start()
    prod_in[home] = prod[r]

    def agg_line(d):
        return remote(
            agg.at[home], agg.at[home], agg_send.at[d - 1], agg_recv.at[d - 1], b, at.across(d)
        )

    for d in (2, 1, 3):
        agg_line(d).start()
    remote(agg.at[home], agg.at[home], agg_send.at[3], agg_sib.at[0], b, sib).start()
    some = prod_in.at[pl.ds(0, nr - 1)]
    remote(some, some, prod_send, prod_recv, b, sib).wait_recv()

    pre[...] = self_pre[...].reshape(rows_blk, width) + prod_in[...].reshape(rows_blk, width)
    upstream = cot_ref[...].astype(F32)
    near_mean = jnp.sum(pre[...], axis=0, keepdims=True) / rows_blk
    off = pre[...] - near_mean
    stat[0:1, :] = near_mean
    stat[1:2, :] = jnp.sum(off * off, axis=0, keepdims=True)
    stat[2:3, :] = jnp.sum(upstream, axis=0, keepdims=True)
    stat[3:4, :] = jnp.sum(upstream * off, axis=0, keepdims=True)
    stat[4:8, :] = jnp.zeros((4, width), F32)
    for d in range(1, nb):
        remote(stat, stats.at[b], stat_send, stat_recv, (b + d) % nb, r).start()
    stats[b] = stat[...]
    some = stats.at[pl.ds(0, nb - 1)]
    remote(some, some, stat_send, stat_recv, b, sib).wait_recv()

    gain, mean_scale = gain_ref[...], scale_ref[...]
    means, cots = stats[:, 0, :], stats[:, 2, :]
    col_mean = jnp.sum(means, axis=0, keepdims=True) / nb
    moved = means - mean_scale * col_mean
    spread = (
        jnp.sum(stats[:, 1, :] + rows_blk * moved * moved, axis=0, keepdims=True) / nodes
    )
    cot_sum = jnp.sum(cots, axis=0, keepdims=True)
    cot_cent = jnp.sum(stats[:, 3, :] + cots * moved, axis=0, keepdims=True)
    col_scale = jnp.sqrt(spread + EPSILON)
    cube = col_scale * col_scale * col_scale
    sharp = gain / col_scale
    weight = gain * cot_cent / (nodes * cube)
    grad_cent_total = sharp * cot_sum - (1.0 - mean_scale) * col_mean * gain * cot_cent / cube
    centered = pre[...] - mean_scale * col_mean
    grad_pre[...] = (
        sharp * upstream - centered * weight - mean_scale * grad_cent_total / nodes
    ).astype(BF16)

    def columns(rep):
        return grad_all.at[:, pl.ds(pl.multiple_of(rep * width, width), width)]

    for d in (2, 1, 3):
        remote(
            grad_pre, columns(r), col_send.at[d - 1], col_recv.at[d - 1], b, at.across(d)
        ).start()
    remote(grad_pre, columns(r), col_send.at[3], col_sib.at[0], b, sib).start()
    grad_all[:, pl.ds(pl.multiple_of(r * width, width), width)] = grad_pre[...]
    normed_ref[...] = (sharp * centered + bias_ref[...]).astype(BF16)
    norm_ref[0:1, :] = cot_cent / col_scale / nodes
    norm_ref[1:2, :] = cot_sum / nodes
    norm_ref[2:3, :] = -col_mean * grad_cent_total / nodes
    for d in (1, 3, 2):
        came = k * NX + (x - d + NX) % NX
        remote(
            agg.at[came], agg.at[came], agg_send.at[d - 1], agg_recv.at[d - 1], b, sib
        ).wait_recv()
        remote(agg.at[came], agg.at[came], agg_send.at[3 + d], agg_sib.at[d], b, sib).start()
    for d in (1, 3, 2):
        came = columns(at.across(NX - d))
        remote(came, came, col_send.at[d - 1], col_recv.at[d - 1], b, sib).wait_recv()
        remote(came, came, col_send.at[3 + d], col_sib.at[d], b, sib).start()
    for d in range(4):
        came = columns(((x - d + NX) % NX) * 2 + (1 - k))
        remote(came, came, col_send.at[3], col_sib.at[d], b, sib).wait_recv()

    def agg_tile(n, carry):
        low = pl.ds(pl.multiple_of(n * COL_TILE, COL_TILE), COL_TILE)
        out = lax.dot_general(
            grad_all[...], w_neigh[low, :], BY_LAST, preferred_element_type=F32
        )
        grad_agg[:, low] = out.astype(BF16)
        return carry

    lax.fori_loop(0, wide // COL_TILE, agg_tile, 0)

    def owed_slab(step, low=0, count=ROW_TILE):
        return cb.at[step, opposite, pl.ds(low, count)]

    def chain_half(w, blk):
        return remote(
            owed_slab(2, w * rows, rows), qside.at[w], chain_send.at[0], chain_recv.at[w], blk, r
        )

    def chain_whole(w, blk):
        return remote(
            owed_slab((1, 3)[w]), qin.at[w], chain_send.at[0], chain_recv.at[2 + w], blk, r
        )

    def chain_shift():
        return remote(
            owed_slab(0), owed, chain_send.at[1], chain_recv.at[4], (b - r + nb) % nb, r
        )

    near = [sib] + [((x + d) % NX) * 2 + j for d in (1, 3) for j in range(2)]
    for step in (2, 1, 3, 0):

        def back_tile(n, carry, step=step):
            cols = pl.ds(pl.multiple_of(n * COL_TILE, COL_TILE), COL_TILE)
            out = lax.dot_general(
                adj[step], grad_agg[:, cols], BY_FIRST, preferred_element_type=F32
            )
            cb[step, :, :, cols] = out.astype(BF16).reshape(NX, ROW_TILE, COL_TILE)
            return carry

        lax.fori_loop(0, wide // COL_TILE, back_tile, 0)
        c = (b - r - nr * step + 2 * nb) % nb
        for goal in near:
            low = pl.multiple_of(goal % 2 * rows, rows)
            remote(
                cb.at[step, goal // 2, pl.ds(low, rows)], pbuf.at[c], back_send, part_recv.at[c], b, goal
            ).start()
        low = pl.multiple_of(k * rows, rows)
        pltpu.make_async_copy(
            cb.at[step, x, pl.ds(low, rows)], pbuf.at[c], back_own.at[step]
        ).start()
        if step == 2:
            chain_half(0, down).start()
            chain_half(1, up).start()
    for d in range(4):
        came = (1 - k) * NX + (x - d + NX) % NX
        remote(agg.at[came], agg.at[came], agg_send.at[3], agg_sib.at[d], b, sib).wait_recv()
    thin = weight_ref.shape[0]
    for n in range(wide // COL_TILE):
        cols = slice(n * COL_TILE, (n + 1) * COL_TILE)
        source = agg[:, :, cols].reshape(rows_blk, COL_TILE)
        out = lax.dot_general(source, grad_pre[...], BY_FIRST, preferred_element_type=F32)
        each = COL_TILE // thin
        term[n * each : (n + 1) * each] = out.astype(BF16).reshape(each, thin, width)
    for d in range(1, nb):
        goal = (b + d) % nb
        remote(term.at[goal], term_in.at[b], term_send, term_recv, goal, r).start()
    term_in[b] = term[b]
    own_rows = pl.ds(pl.multiple_of(r * rows, rows), rows)
    self_rows[...] = lax.dot_general(
        grad_all[own_rows, :], w_self[...], BY_LAST, preferred_element_type=F32
    )
    for w, blk in ((0, down), (1, up)):
        step = (1, 3)[w]
        part = pl.ds(w * rows, rows)
        chain_half(w, blk).wait_recv()
        cb[step, opposite, part] = (
            cb[step, opposite, part].astype(F32) + qside[w].astype(F32)
        ).astype(BF16)
        chain_whole(w, blk).start()
    for step in range(steps):
        c = (b - r - nr * step + 2 * nb) % nb
        pltpu.make_async_copy(pbuf.at[c], pbuf.at[c], back_own.at[step]).wait()

    def chain_sum():
        for w, blk in ((0, down), (1, up)):
            chain_whole(w, blk).wait_recv()
        cb[0, opposite] = (
            cb[0, opposite].astype(F32) + qin[0].astype(F32) + qin[1].astype(F32)
        ).astype(BF16)

        @pl.when(r != 0)
        def _():
            chain_shift().start()

        @pl.when(r == 0)
        def _():
            owed[...] = cb[0, opposite]

    def lend(j):
        return remote(
            owed.at[pl.ds(j * rows, rows)], lent.at[k], lent_send, lent_recv.at[k], b, opposite * 2 + j
        )

    def chain_lend():
        @pl.when(r != 0)
        def _():
            chain_shift().wait_recv()

        for j in range(2):
            lend(j).start()

    def own(dy, dz):
        c = at.block(dy, dz)
        source = (b - c + nb) % nr

        @pl.when((source != r) & (source // 2 != opposite))
        def _():
            remote(pbuf.at[c], pbuf.at[c], back_send, part_recv.at[c], b, r).wait_recv()

        @pl.when(source // 2 == opposite)
        def _():
            pbuf[c] = jnp.zeros((rows, wide), BF16)

        return c

    BACK = [reach] + [dz for t in range(reach - 1, 0, -1) for dz in (t, -t)] + [0]

    def back_far(i):
        c = own(2, BACK[i])
        for w, way in ((0, 1), (1, -1)):
            part = pl.ds(w * half, half)
            remote(
                pbuf.at[c, part], yh.at[w, i], back_line, h_recv.at[w, i], at.block(way, 0), r
            ).start()

    def back_side(i):
        for w, way in ((0, 1), (1, -1)):
            c = own(way, BACK[i])
            remote(yh.at[w, i], yh.at[w, i], back_line, h_recv.at[w, i], b, r).wait_recv()
            part = pl.ds(w * half, half)
            pbuf[c, part] = (pbuf[c, part].astype(F32) + yh[w, i].astype(F32)).astype(BF16)
            remote(
                pbuf.at[c], yr.at[w, i], back_line, y_recv.at[w, i], at.block(way, 0), r
            ).start()

    def z_send(c, w, t, low=0, count=rows):
        part = pl.ds(low, count)
        return remote(
            pbuf.at[c, part], zr.at[w, t, part], back_line, z_recv.at[w, t], at.block(0, (1, -1)[w]), r
        )

    def back_column(i):
        dz = BACK[i]
        c = own(0, dz)
        for w in range(2):
            remote(yr.at[w, i], yr.at[w, i], back_line, y_recv.at[w, i], b, r).wait_recv()
        value = pbuf[c].astype(F32) + yr[0, i].astype(F32) + yr[1, i].astype(F32)
        if dz == reach:
            pbuf[c] = value.astype(BF16)
            for w in range(2):
                z_send(c, w, reach - 1, w * half, half).start()
            return None
        if dz == 0:
            for w in range(2):
                z_send(c, w, 0).wait_recv()
                value = value + zr[w, 0].astype(F32)
            return value
        w, t = (0, dz) if dz > 0 else (1, -dz)
        if t == reach - 1:
            low = w * half
            z_send(c, w, t, low, half).wait_recv()
            pbuf[c] = value.astype(BF16)
            part = pl.ds(low, half)
            pbuf[c, part] = (value[low : low + half] + zr[w, t, part].astype(F32)).astype(BF16)
        else:
            z_send(c, w, t).wait_recv()
            pbuf[c] = (value + zr[w, t].astype(F32)).astype(BF16)
        z_send(c, w, t - 1).start()
        return None

    for i in range(nz + 2):
        if i < nz:
            back_far(i)
        if 1 <= i < nz + 1:
            back_side(i - 1)
        if i >= 2:
            value = back_column(i - 2)
        if i == 3:
            chain_sum()
        if i == 6:
            chain_lend()
    for j in range(2):
        remote(lent.at[j], lent.at[j], lent_send, lent_recv.at[j], b, r).wait_recv()
        value = value + lent[j].astype(F32)
    out_ref[...] = (value + self_rows[...]).astype(BF16)

    some = term_in.at[pl.ds(0, nb - 1)]
    remote(some, some, term_send, term_recv, b, sib).wait()
    weight_ref[...] = jnp.sum(term_in[...].astype(F32), axis=0) / nodes

    def sent(some, sem):
        remote(some, some, sem, term_recv, b, sib).wait_send()

    sent(g.at[pl.ds(0, 3 + 4 * (nz - 1))], line_send)
    sent(g.at[pl.ds(0, steps * (nr - 3))], swap_send)
    sent(o.at[0, pl.ds(0, NX - 1)], plane_send.at[0])
    sent(cb.at[0, pl.ds(0, NX - 1)], chain_send.at[0])

    @pl.when(r != 0)
    def _():
        shift_out().wait_send()
        chain_shift().wait_send()

    sent(lent, lent_send)
    sent(pbuf.at[pl.ds(0, 3 + 4 * (nz - 1))], back_line)
    sent(pbuf.at[pl.ds(0, steps * (nr - 3))], back_send)
    sent(pb, red_send.at[0])
    for d in range(1, NX):
        sent(qb.at[d - 1], red_send.at[d])
    for i in range(7):
        sent(agg.at[0], agg_send.at[i])
        sent(grad_pre, col_send.at[i])
    sent(prod_in.at[pl.ds(0, nr - 1)], prod_send)
    sent(stats.at[pl.ds(0, nb - 1)], stat_send)


def body(
    features,
    node_order,
    adj_tiles,
    counts,
    coords,
    w_self,
    w_neigh,
    norm_gain,
    norm_bias,
    mean_scale,
    cotangent,
):
    nb, nr = lax.axis_size("blk"), lax.axis_size("rep")
    rows_blk, wide = features.shape
    width = cotangent.shape[1]
    rows = rows_blk // nr
    thin = wide // nb
    steps = nb // nr
    nz = nb // NY
    reach = nz // 2
    tiles = adj_tiles[0, 0]
    dma = pltpu.SemaphoreType.DMA
    vmem = pl.BlockSpec(memory_space=pltpu.VMEM)
    smem = pl.BlockSpec(memory_space=pltpu.SMEM)
    hbm = pl.BlockSpec(memory_space=pl.ANY)

    def room(*shape, dtype=BF16):
        return pltpu.VMEM(shape, dtype)

    return tuple(
        pl.pallas_call(
            layer_kernel,
            out_shape=(
                jax.ShapeDtypeStruct((rows_blk, width), BF16),
                jax.ShapeDtypeStruct((rows, wide), BF16),
                jax.ShapeDtypeStruct((thin, width), F32),
                jax.ShapeDtypeStruct((3, width), F32),
            ),
            in_specs=[hbm, vmem, hbm, smem, smem, hbm, hbm, vmem, vmem, vmem, vmem],
            out_specs=(vmem,) * 4,
            scratch_shapes=[
                room(rows_blk, wide),
                room(*tiles.shape),
                room(wide, wide),
                room(wide, wide),
                dma((4,)),
                room(NX, ROW_TILE, wide),
                room(steps, rows_blk, rows_blk),
                room(NX, ROW_TILE, width, dtype=F32),
                room(nb, rows, wide),
                room(steps, NX, ROW_TILE, wide),
                room(rows_blk, wide, dtype=F32),
                room(NX, rows, wide),
                room(NX, rows, wide),
                room(NX - 1, rows, wide),
                room(NX - 1, rows, wide),
                room(nr, rows, wide),
                room(nr, rows, width, dtype=F32),
                room(nr, rows, width, dtype=F32),
                room(rows_blk, width, dtype=F32),
                room(8, width, dtype=F32),
                room(nb, 8, width, dtype=F32),
                room(rows_blk, width),
                room(rows_blk, wide),
                room(rows_blk, wide),
                room(rows, wide, dtype=F32),
                room(nb, thin, width),
                room(nb, thin, width),
                room(steps, NX, ROW_TILE, wide),
                room(nb, rows, wide),
                room(2, reach, rows, wide),
                room(2, nz, rows, wide),
                room(2, nz, rows // 2, wide),
                room(2, ROW_TILE, wide),
                room(2, rows, wide),
                room(ROW_TILE, wide),
                room(2, rows, wide),
                dma((nz + 1,)),
                dma((4, nz)),
                dma((2,)),
                dma((5,)),
                dma(()),
                dma(()),
                dma((steps,)),
                dma((steps,)),
                dma((4,)),
                dma(()),
                dma((3,)),
                dma(()),
                dma(()),
                dma((7,)),
                dma((3,)),
                dma((4,)),
                dma(()),
                dma(()),
                dma((7,)),
                dma((3,)),
                dma((4,)),
                dma(()),
                dma(()),
                dma((steps,)),
                dma(()),
                dma((nb,)),
                dma(()),
                dma((2, reach)),
                dma((2, nz)),
                dma((2, nz)),
                dma((2,)),
                dma((5,)),
                dma(()),
                dma((2,)),
            ],
            compiler_params=pltpu.CompilerParams(
                collective_id=0, has_side_effects=True, vmem_limit_bytes=56 << 20
            ),
            name="layer",
        )(
            features,
            node_order.reshape(1, rows_blk),
            tiles,
            counts.reshape(steps),
            coords[0, 0],
            w_self,
            w_neigh,
            norm_gain.reshape(1, width),
            norm_bias.reshape(1, width),
            mean_scale.reshape(1, width),
            cotangent,
        )
    )


def solution(mesh):
    in_specs = (
        P("blk", None),
        P("blk"),
        P("blk", "rep", None, None, None, None),
        P("blk", "rep", None),
        P("blk", "rep", None, None, None),
        P(),
        P(),
        P("rep"),
        P("rep"),
        P("rep"),
        P("blk", "rep"),
    )
    out_specs = (P("blk", "rep"), P(("blk", "rep"), None), P("blk", "rep"), P(None, "rep"))
    return jax.shard_map(body, mesh=mesh, in_specs=in_specs, out_specs=out_specs, check_vma=False)
```

```python
import jax
import jax.numpy as jnp
from jax import lax
from jax.experimental import pallas as pl
from jax.experimental.pallas import tpu as pltpu
from jax.sharding import PartitionSpec as P

EPSILON = 1e-05
MESH = pl.DeviceIdType.MESH
NY = 4
NX = 4
BF16 = jnp.bfloat16
F32 = jnp.float32


def remote(src, dst, send_sem, recv_sem, blk, rep):
    return pltpu.make_async_remote_copy(
        src_ref=src,
        dst_ref=dst,
        send_sem=send_sem,
        recv_sem=recv_sem,
        device_id=(blk, rep),
        device_id_type=MESH,
    )


def greet(peers):
    barrier = pltpu.get_barrier_semaphore()
    for blk, rep in peers:
        pl.semaphore_signal(barrier, inc=1, device_id=(blk, rep), device_id_type=MESH)


def greeted(count):
    pl.semaphore_wait(pltpu.get_barrier_semaphore(), count)


class Place:
    def __init__(self):
        self.b = lax.axis_index("blk")
        self.r = lax.axis_index("rep")
        self.nb = lax.axis_size("blk")
        self.nr = lax.axis_size("rep")
        self.nz = self.nb // NY
        self.y = self.b % NY
        self.z = self.b // NY
        self.x = self.r // 2
        self.k = self.r % 2
        self.sib = self.x * 2 + (1 - self.k)

    def block(self, dy, dz):
        return ((self.z + dz + self.nz) % self.nz) * NY + (self.y + dy + NY) % NY

    def across(self, dx):
        return ((self.x + dx) % NX) * 2 + self.k

    def rep_peers(self):
        return [(self.b, (self.r + d) % self.nr) for d in range(1, self.nr)]


ROW_TILE = 128
COL_TILE = 256
BY_FIRST = (((0,), (0,)), ((), ()))
BY_LAST = (((1,), (1,)), ((), ()))


def layer_kernel(
    feat_hbm,
    order_ref,
    tiles_hbm,
    counts_ref,
    coords_ref,
    self_hbm,
    neigh_hbm,
    gain_ref,
    bias_ref,
    scale_ref,
    cot_ref,
    normed_ref,
    out_ref,
    weight_ref,
    norm_ref,
    feat,
    tiles,
    w_self,
    w_neigh,
    load_sem,
    reordered,
    adj,
    self_pre,
    g,
    o,
    acc,
    pb,
    rb1,
    qb,
    rb2,
    rb3,
    agg,
    prod,
    prod_in,
    pre,
    stat,
    stats_y,
    line_stat,
    stats,
    grad_pre,
    grad_all,
    grad_agg,
    self_rows,
    term,
    term_in,
    term_mid,
    term_last,
    cb,
    pbuf,
    zr,
    yr,
    yh,
    qin,
    qside,
    owed,
    lent,
    line_recv,
    side_recv,
    plane_send,
    plane_recv,
    line_send,
    swap_send,
    swap_recv,
    own_sem,
    red_send,
    red_recv1,
    red_recv2,
    prod_send,
    prod_recv,
    agg_send,
    agg_recv,
    stat_send,
    stat_recv,
    col_send,
    col_recv,
    term_send,
    term_recv,
    back_own,
    back_send,
    part_recv,
    back_line,
    z_recv,
    y_recv,
    h_recv,
    chain_send,
    chain_recv,
    lent_send,
    lent_recv,
):
    at = Place()
    b, r, nb, nr, nz = at.b, at.r, at.nb, at.nr, at.nz
    x, k, sib = at.x, at.k, at.sib
    rows, wide = out_ref.shape
    half = rows // 2
    rows_blk = rows * nr
    width = cot_ref.shape[1]
    nodes = rows_blk * nb
    reach = nz // 2
    sides = rows_blk // tiles.shape[-1]
    side = tiles.shape[-1]
    slots = tiles.shape[1]
    steps = nb // nr

    loads = [
        pltpu.make_async_copy(src, dst, load_sem.at[i])
        for i, (src, dst) in enumerate(
            ((feat_hbm, feat), (tiles_hbm, tiles), (self_hbm, w_self), (neigh_hbm, w_neigh))
        )
    ]
    for load in loads:
        load.start()

    def reorder(low):
        ids = lax.broadcasted_iota(jnp.int32, (rows_blk, ROW_TILE), 0)
        want = order_ref[:, pl.ds(pl.multiple_of(low, ROW_TILE), ROW_TILE)]
        pick = jnp.where(ids == want, 1.0, 0.0).astype(BF16)
        return lax.dot_general(pick, feat[...], BY_FIRST, preferred_element_type=F32).astype(BF16)

    peers = [((b + d) % nb, r) for d in range(1, nb)] + at.rep_peers()
    greet(peers)
    loads[0].wait()
    reordered[x] = reorder(x * ROW_TILE)
    g[b] = reordered[x, pl.ds(pl.multiple_of(k * rows, rows), rows), :]
    greeted(len(peers))
    opposite = (x + 2) % NX
    far_blk = nb // steps

    def pass_on(c, sem, blk, low=0, count=rows):
        part = pl.ds(low, count)
        return remote(g.at[c, part], g.at[c, part], line_send, sem, blk, r)

    def hand_out(dy, dz):
        c = at.block(dy, dz)
        diff = (b - c + nb) % nb
        goal = diff % nr
        step = diff // nr
        slot = o.at[step, x, pl.ds(pl.multiple_of(k * rows, rows), rows)]

        @pl.when((goal != r) & (goal // 2 != opposite))
        def _():
            remote(g.at[c], slot, swap_send, swap_recv.at[step], b, goal).start()

        @pl.when(goal == r)
        def _():
            pltpu.make_async_copy(g.at[c], slot, own_sem.at[step]).start()

    def fill_block(step):
        def run():
            if step == 0:
                loads[1].wait()
            for i in range(sides):
                for j in range(sides):
                    block = jnp.zeros((side, side), F32)
                    for t in range(slots):
                        live = (
                            (t < counts_ref[step])
                            & (coords_ref[step, t, 0] == i)
                            & (coords_ref[step, t, 1] == j)
                        )
                        chosen = jnp.where(live, 1.0, 0.0)
                        block = block + chosen * tiles[step, t].astype(F32)
                    adj[step, i * side : (i + 1) * side, j * side : (j + 1) * side] = block.astype(BF16)

        return run

    def fill_rows(d):
        def run():
            n = (x + d) % NX
            if d % 2:
                reordered[n] = reorder(n * ROW_TILE)
            if d == 0:
                loads[2].wait()
            cols = pl.ds(pl.multiple_of(r * width, width), width)
            self_pre[n] = jnp.dot(reordered[n], w_self[:, cols], preferred_element_type=F32)

        return run

    work = [fill_block(step) for step in range(steps)] + [fill_rows(d) for d in range(NX)]

    def slab(step, low=0, count=ROW_TILE):
        return o.at[step, opposite, pl.ds(low, count)]

    def relay(step_from, step_to, sem, blk, low=0, count=ROW_TILE):
        return remote(
            slab(step_from, low, count), slab(step_to, low, count), plane_send.at[0], plane_recv.at[sem], blk, r
        )

    def shift_out():
        return remote(
            reordered.at[opposite], slab(0), plane_send.at[1], plane_recv.at[0], (b + r) % nb, r
        )

    up, down = (b + far_blk) % nb, (b - far_blk + nb) % nb

    def plane_start():
        @pl.when(r != 0)
        def _():
            shift_out().start()

        @pl.when(r == 0)
        def _():
            o[0, opposite] = reordered[opposite]

    def plane_spread():
        @pl.when(r != 0)
        def _():
            shift_out().wait_recv()

        relay(0, 1, 1, up).start()
        relay(0, 3, 3, down).start()

    def plane_far():
        relay(0, 1, 1, up).wait_recv()
        relay(1, 2, 2, up, 0, rows).start()
        relay(0, 3, 3, down).wait_recv()
        relay(3, 2, 4, down, rows, rows).start()

    def plane_end():
        relay(1, 2, 2, up, 0, rows).wait_recv()
        relay(3, 2, 4, down, rows, rows).wait_recv()

    ORDER = [0] + [dz for t in range(1, reach) for dz in (-t, t)] + [reach]

    def column_step(i):
        dz = ORDER[i]
        c = at.block(0, dz)
        if dz == reach:
            for w in range(2):
                pass_on(c, line_recv.at[reach + w], b, w * half, half).wait_recv()
        elif dz:
            pass_on(c, line_recv.at[dz % nz + (dz < 0)], b).wait_recv()
        for w, way in ((0, 1), (1, -1)):
            if dz == 0 or (dz * way < 0 and abs(dz) < reach - 1):
                n = (dz - way) % nz
                pass_on(c, line_recv.at[n + (n > reach)], at.block(0, way)).start()
            elif dz * way == 1 - reach:
                pass_on(c, line_recv.at[reach + w], at.block(0, way), w * half, half).start()
        for w, way in ((0, 1), (1, -1)):
            pass_on(c, side_recv.at[w, i], at.block(way, 0)).start()
        hand_out(0, dz)

    def side_step(i):
        dz = ORDER[i]
        for w, way in ((0, 1), (1, -1)):
            c = at.block(-way, dz)
            pass_on(c, side_recv.at[w, i], b).wait_recv()
            pass_on(c, side_recv.at[2 + w, i], at.block(way, 0), w * half, half).start()
            hand_out(-way, dz)

    def far_step(i):
        dz = ORDER[i]
        c = at.block(2, dz)
        for w in range(2):
            pass_on(c, side_recv.at[2 + w, i], b, w * half, half).wait_recv()
        hand_out(2, dz)

    lag = 2
    for i in range(nz + lag + 1):
        if i < nz:
            column_step(i)
        if i == 0:
            reordered[opposite] = reorder(opposite * ROW_TILE)
            plane_start()
        if lag <= i < nz + lag:
            side_step(i - lag)
        if lag < i:
            far_step(i - lag - 1)
        if i == 4:
            plane_spread()
        if i == 8:
            plane_far()
        if i >= 2:
            if work:
                work.pop(0)()
    plane_end()

    for i, step in enumerate((0, 1, 3, 2)):
        some = o.at[step, 0, pl.ds(0, rows)]
        pltpu.make_async_copy(some, some, own_sem.at[step]).wait()
        some = g.at[pl.ds(0, nr - 3)]
        remote(some, some, swap_send, swap_recv.at[step], b, r).wait_recv()

        def part_tile(n, carry, step=step, i=i):
            cols = pl.ds(pl.multiple_of(n * COL_TILE, COL_TILE), COL_TILE)
            source = o[step, :, :, cols].reshape(rows_blk, COL_TILE)
            out = jnp.dot(adj[step], source, preferred_element_type=F32)
            acc[:, cols] = out if i == 0 else acc[:, cols] + out
            return carry

        lax.fori_loop(0, wide // COL_TILE, part_tile, 0)

    def chunk(m):
        return acc[pl.ds(pl.multiple_of(m * rows, rows), rows), :]

    def to_sibling(m):
        return remote(pb.at[m], rb1.at[m], red_send.at[0], red_recv1.at[m], b, sib)

    def both(m):
        return chunk(k * NX + m) + rb1[m].astype(F32)

    turns = [(x + d) % NX for d in (2, 1, 3, 0)]
    for m in turns:
        pb[m] = chunk((1 - k) * NX + m).astype(BF16)
        to_sibling(m).start()
    loads[3].wait()

    def half_way(w):
        part = pl.ds(w * half, half)
        return remote(
            qb.at[0, part], rb3.at[w], red_send.at[1], red_recv2.at[w], b, at.across((1, 3)[w])
        )

    def one_way(w):
        return remote(
            qb.at[1 + w], rb2.at[w], red_send.at[1], red_recv2.at[2 + w], b, at.across((1, 3)[w])
        )

    to_sibling(turns[0]).wait_recv()
    qb[0] = both(turns[0]).astype(BF16)
    for w in range(2):
        half_way(w).start()
    for w in range(2):
        to_sibling(turns[1 + w]).wait_recv()
        value = both(turns[1 + w])
        qb[1 + w] = value.astype(BF16)
        half_way(w).wait_recv()
        part = pl.ds(w * half, half)
        qb[1 + w, part] = (value[w * half : (w + 1) * half] + rb3[w].astype(F32)).astype(BF16)
        one_way(w).start()
    home = k * NX + x
    to_sibling(x).wait_recv()
    total = both(x)
    for w in range(2):
        one_way(w).wait_recv()
        total = total + rb2[w].astype(F32)
    agg[home] = total.astype(BF16)

    for n in range(wide // COL_TILE):
        cols = slice(n * COL_TILE, (n + 1) * COL_TILE)
        out = jnp.dot(agg[home], w_neigh[:, cols], preferred_element_type=F32)
        for j in range(COL_TILE // width):
            prod[n * (COL_TILE // width) + j] = out[:, j * width : (j + 1) * width].astype(BF16)
    for d in (4, 5, 2, 3, 6, 7, 1):
        goal = (r + d) % nr
        remote(prod.at[goal], prod_in.at[home], prod_send, prod_recv, b, goal).start()
    prod_in[home] = prod[r]

    class Line:
        def __init__(self, ref, tall, send, recv):
            self.ref, self.tall, self.send, self.recv = ref, tall, send, recv

        def move(self, chip, core, sem, goal, low=0, count=None):
            ref = self.ref(chip, core, low, self.tall if count is None else count)
            return remote(ref, ref, self.send, self.recv.at[sem], b, goal)

        def begin(self):
            self.move(x, k, 4, sib).start()
            self.move(x, k, 0, at.across(1)).start()
            self.move(x, k, 1, at.across(3)).start()

        def middle(self):
            side = self.tall // 2
            for w, d in ((0, 3), (1, 1)):
                chip = (x + d) % NX
                self.move(chip, k, w, sib).wait_recv()
                self.move(chip, k, 2 + w, at.across(4 - d), w * side, side).start()
                self.move(chip, k, 5 + w, sib).start()

        def end(self):
            side = self.tall // 2
            chip = (x + 2) % NX
            for w in range(2):
                self.move(chip, k, 2 + w, sib, w * side, side).wait_recv()
            self.move(chip, k, 7, sib).start()

        def wait(self):
            for i, d in enumerate((0, 3, 1, 2)):
                self.move((x + d) % NX, 1 - k, 4 + i, sib).wait_recv()

    def agg_chunk(chip, core, low, count):
        return agg.at[core * NX + chip, pl.ds(low, count)]

    def grad_chunk(chip, core, low, count):
        cols = pl.ds(pl.multiple_of((chip * 2 + core) * width, width), width)
        return grad_all.at[pl.ds(low, count), cols]

    agg_line = Line(agg_chunk, rows, agg_send, agg_recv)
    grad_line = Line(grad_chunk, rows_blk, col_send, col_recv)
    agg_line.begin()
    some = prod_in.at[pl.ds(0, nr - 1)]
    remote(some, some, prod_send, prod_recv, b, sib).wait_recv()

    pre[...] = self_pre[...].reshape(rows_blk, width) + prod_in[...].astype(F32).reshape(
        rows_blk, width
    )
    upstream = cot_ref[...].astype(F32)
    near_mean = jnp.sum(pre[...], axis=0, keepdims=True) / rows_blk
    off = pre[...] - near_mean
    stat[0:1, :] = near_mean
    stat[1:2, :] = jnp.sum(off * off, axis=0, keepdims=True)
    stat[2:3, :] = jnp.sum(upstream, axis=0, keepdims=True)
    stat[3:4, :] = jnp.sum(upstream * off, axis=0, keepdims=True)
    stat[4:8, :] = jnp.zeros((4, width), F32)
    stats_y[at.y] = stat[...]
    for d in (2, 1, 3):
        remote(
            stat, stats_y.at[at.y], stat_send.at[0], stat_recv.at[0], at.block(d, 0), r
        ).start()
    some = stats_y.at[pl.ds(0, NY - 1)]
    remote(some, some, stat_send.at[0], stat_recv.at[0], b, sib).wait_recv()
    line_means, line_cots = stats_y[:, 0, :], stats_y[:, 2, :]
    line_mean = jnp.sum(line_means, axis=0, keepdims=True) / NY
    apart = line_means - line_mean
    line_stat[0:1, :] = line_mean
    line_stat[1:2, :] = jnp.sum(
        stats_y[:, 1, :] + rows_blk * apart * apart, axis=0, keepdims=True
    )
    line_stat[2:3, :] = jnp.sum(line_cots, axis=0, keepdims=True)
    line_stat[3:4, :] = jnp.sum(stats_y[:, 3, :] + line_cots * apart, axis=0, keepdims=True)
    line_stat[4:8, :] = jnp.zeros((4, width), F32)
    stats[at.z] = line_stat[...]
    for d in (4, 3, 5, 2, 6, 1, 7):
        remote(
            line_stat, stats.at[at.z], stat_send.at[1], stat_recv.at[1], at.block(0, d), r
        ).start()
    some = stats.at[pl.ds(0, nz - 1)]
    remote(some, some, stat_send.at[1], stat_recv.at[1], b, sib).wait_recv()

    gain, mean_scale = gain_ref[...], scale_ref[...]
    means, cots = stats[:, 0, :], stats[:, 2, :]
    col_mean = jnp.sum(means, axis=0, keepdims=True) / nz
    moved = means - mean_scale * col_mean
    spread = (
        jnp.sum(stats[:, 1, :] + NY * rows_blk * moved * moved, axis=0, keepdims=True) / nodes
    )
    cot_sum = jnp.sum(cots, axis=0, keepdims=True)
    cot_cent = jnp.sum(stats[:, 3, :] + cots * moved, axis=0, keepdims=True)
    col_scale = jnp.sqrt(spread + EPSILON)
    cube = col_scale * col_scale * col_scale
    sharp = gain / col_scale
    weight = gain * cot_cent / (nodes * cube)
    grad_cent_total = sharp * cot_sum - (1.0 - mean_scale) * col_mean * gain * cot_cent / cube
    centered = pre[...] - mean_scale * col_mean
    grad_pre[...] = (
        sharp * upstream - centered * weight - mean_scale * grad_cent_total / nodes
    ).astype(BF16)

    grad_all[:, pl.ds(pl.multiple_of(r * width, width), width)] = grad_pre[...]
    grad_line.begin()
    normed_ref[...] = (sharp * centered + bias_ref[...]).astype(BF16)
    norm_ref[0:1, :] = cot_cent / col_scale / nodes
    norm_ref[1:2, :] = cot_sum / nodes
    norm_ref[2:3, :] = -col_mean * grad_cent_total / nodes
    agg_line.middle()
    grad_line.middle()
    agg_line.end()
    grad_line.end()
    grad_line.wait()

    def agg_tile(n, carry):
        low = pl.ds(pl.multiple_of(n * COL_TILE, COL_TILE), COL_TILE)
        out = lax.dot_general(
            grad_all[...], w_neigh[low, :], BY_LAST, preferred_element_type=F32
        )
        grad_agg[:, low] = out.astype(BF16)
        return carry

    lax.fori_loop(0, wide // COL_TILE, agg_tile, 0)

    def term_y():
        agg_line.wait()
        thin = weight_ref.shape[0]
        for n in range(wide // COL_TILE):
            cols = slice(n * COL_TILE, (n + 1) * COL_TILE)
            source = agg[:, :, cols].reshape(rows_blk, COL_TILE)
            out = lax.dot_general(source, grad_pre[...], BY_FIRST, preferred_element_type=F32)
            each = COL_TILE // thin
            for j in range(each):
                at_z, at_y = divmod(n * each + j, NY)
                term[at_y, at_z] = out[j * thin : (j + 1) * thin].astype(BF16)
        for d in (2, 1, 3):
            goal = (at.y + d) % NY
            remote(
                term.at[goal], term_in.at[at.y], term_send.at[0], term_recv.at[0], at.block(d, 0), r
            ).start()
        term_in[at.y] = term[at.y]

    def term_z():
        some = term_in.at[pl.ds(0, NY - 1)]
        remote(some, some, term_send.at[0], term_recv.at[0], b, sib).wait_recv()
        term_mid[...] = jnp.sum(term_in[...].astype(F32), axis=0).astype(BF16)
        for d in (4, 3, 5, 2, 6, 1, 7):
            goal = (at.z + d) % nz
            remote(
                term_mid.at[goal], term_last.at[at.z], term_send.at[1], term_recv.at[1], at.block(0, d), r
            ).start()
        term_last[at.z] = term_mid[at.z]

    def owed_slab(step, low=0, count=ROW_TILE):
        return cb.at[step, opposite, pl.ds(low, count)]

    def chain_half(w, blk):
        return remote(
            owed_slab(2, w * rows, rows), qside.at[w], chain_send.at[0], chain_recv.at[w], blk, r
        )

    def chain_whole(w, blk):
        return remote(
            owed_slab((1, 3)[w]), qin.at[w], chain_send.at[0], chain_recv.at[2 + w], blk, r
        )

    def chain_shift():
        return remote(
            owed_slab(0), owed, chain_send.at[1], chain_recv.at[4], (b - r + nb) % nb, r
        )

    near = [sib] + [((x + d) % NX) * 2 + j for d in (1, 3) for j in range(2)]
    for step in (2, 1, 3, 0):

        def back_tile(n, carry, step=step):
            cols = pl.ds(pl.multiple_of(n * COL_TILE, COL_TILE), COL_TILE)
            out = lax.dot_general(
                adj[step], grad_agg[:, cols], BY_FIRST, preferred_element_type=F32
            )
            cb[step, :, :, cols] = out.astype(BF16).reshape(NX, ROW_TILE, COL_TILE)
            return carry

        lax.fori_loop(0, wide // COL_TILE, back_tile, 0)
        c = (b - r - nr * step + 2 * nb) % nb
        for goal in near:
            low = pl.multiple_of(goal % 2 * rows, rows)
            remote(
                cb.at[step, goal // 2, pl.ds(low, rows)], pbuf.at[c], back_send, part_recv.at[c], b, goal
            ).start()
        low = pl.multiple_of(k * rows, rows)
        pltpu.make_async_copy(
            cb.at[step, x, pl.ds(low, rows)], pbuf.at[c], back_own.at[step]
        ).start()
        if step == 2:
            chain_half(0, down).start()
            chain_half(1, up).start()
    term_y()
    own_rows = pl.ds(pl.multiple_of(r * rows, rows), rows)
    self_rows[...] = lax.dot_general(
        grad_all[own_rows, :], w_self[...], BY_LAST, preferred_element_type=F32
    )
    for w, blk in ((0, down), (1, up)):
        step = (1, 3)[w]
        part = pl.ds(w * rows, rows)
        chain_half(w, blk).wait_recv()
        cb[step, opposite, part] = (
            cb[step, opposite, part].astype(F32) + qside[w].astype(F32)
        ).astype(BF16)
        chain_whole(w, blk).start()
    for step in range(steps):
        c = (b - r - nr * step + 2 * nb) % nb
        pltpu.make_async_copy(pbuf.at[c], pbuf.at[c], back_own.at[step]).wait()

    def chain_sum():
        for w, blk in ((0, down), (1, up)):
            chain_whole(w, blk).wait_recv()
        cb[0, opposite] = (
            cb[0, opposite].astype(F32) + qin[0].astype(F32) + qin[1].astype(F32)
        ).astype(BF16)

        @pl.when(r != 0)
        def _():
            chain_shift().start()

        @pl.when(r == 0)
        def _():
            owed[...] = cb[0, opposite]

    def lend(j):
        return remote(
            owed.at[pl.ds(j * rows, rows)], lent.at[k], lent_send, lent_recv.at[k], b, opposite * 2 + j
        )

    def chain_lend():
        @pl.when(r != 0)
        def _():
            chain_shift().wait_recv()

        for j in range(2):
            lend(j).start()

    def own(dy, dz):
        c = at.block(dy, dz)
        source = (b - c + nb) % nr

        @pl.when((source != r) & (source // 2 != opposite))
        def _():
            remote(pbuf.at[c], pbuf.at[c], back_send, part_recv.at[c], b, r).wait_recv()

        @pl.when(source // 2 == opposite)
        def _():
            pbuf[c] = jnp.zeros((rows, wide), BF16)

        return c

    BACK = [reach] + [dz for t in range(reach - 1, 0, -1) for dz in (t, -t)] + [0]

    def back_far(i):
        c = own(2, BACK[i])
        for w, way in ((0, 1), (1, -1)):
            part = pl.ds(w * half, half)
            remote(
                pbuf.at[c, part], yh.at[w, i], back_line, h_recv.at[w, i], at.block(way, 0), r
            ).start()

    def back_side(i):
        for w, way in ((0, 1), (1, -1)):
            c = own(way, BACK[i])
            remote(yh.at[w, i], yh.at[w, i], back_line, h_recv.at[w, i], b, r).wait_recv()
            part = pl.ds(w * half, half)
            pbuf[c, part] = (pbuf[c, part].astype(F32) + yh[w, i].astype(F32)).astype(BF16)
            remote(
                pbuf.at[c], yr.at[w, i], back_line, y_recv.at[w, i], at.block(way, 0), r
            ).start()

    def z_send(c, w, t, low=0, count=rows):
        part = pl.ds(low, count)
        return remote(
            pbuf.at[c, part], zr.at[w, t, part], back_line, z_recv.at[w, t], at.block(0, (1, -1)[w]), r
        )

    def back_column(i):
        dz = BACK[i]
        c = own(0, dz)
        for w in range(2):
            remote(yr.at[w, i], yr.at[w, i], back_line, y_recv.at[w, i], b, r).wait_recv()
        value = pbuf[c].astype(F32) + yr[0, i].astype(F32) + yr[1, i].astype(F32)
        if dz == reach:
            pbuf[c] = value.astype(BF16)
            for w in range(2):
                z_send(c, w, reach - 1, w * half, half).start()
            return None
        if dz == 0:
            for w in range(2):
                z_send(c, w, 0).wait_recv()
                value = value + zr[w, 0].astype(F32)
            return value
        w, t = (0, dz) if dz > 0 else (1, -dz)
        if t == reach - 1:
            low = w * half
            z_send(c, w, t, low, half).wait_recv()
            pbuf[c] = value.astype(BF16)
            part = pl.ds(low, half)
            pbuf[c, part] = (value[low : low + half] + zr[w, t, part].astype(F32)).astype(BF16)
        else:
            z_send(c, w, t).wait_recv()
            pbuf[c] = (value + zr[w, t].astype(F32)).astype(BF16)
        z_send(c, w, t - 1).start()
        return None

    for i in range(nz + 4):
        if i < nz:
            back_far(i)
        if 2 <= i < nz + 2:
            back_side(i - 2)
        if i >= 4:
            value = back_column(i - 4)
        if i == 4:
            chain_sum()
        if i == 5:
            term_z()
        if i == 7:
            chain_lend()
    for j in range(2):
        remote(lent.at[j], lent.at[j], lent_send, lent_recv.at[j], b, r).wait_recv()
        value = value + lent[j].astype(F32)
    out_ref[...] = (value + self_rows[...]).astype(BF16)

    some = term_last.at[pl.ds(0, nz - 1)]
    remote(some, some, term_send.at[1], term_recv.at[1], b, sib).wait_recv()
    weight_ref[...] = jnp.sum(term_last[...].astype(F32), axis=0) / nodes

    def sent(some, sem):
        remote(some, some, sem, term_recv.at[0], b, sib).wait_send()

    sent(g.at[pl.ds(0, 3 + 4 * (nz - 1))], line_send)
    sent(g.at[pl.ds(0, steps * (nr - 3))], swap_send)
    sent(o.at[0, pl.ds(0, NX - 1)], plane_send.at[0])
    sent(cb.at[0, pl.ds(0, NX - 1)], chain_send.at[0])

    @pl.when(r != 0)
    def _():
        shift_out().wait_send()
        chain_shift().wait_send()

    sent(lent, lent_send)
    sent(pbuf.at[pl.ds(0, 3 + 4 * (nz - 1))], back_line)
    sent(pbuf.at[pl.ds(0, steps * (nr - 3))], back_send)
    sent(pb, red_send.at[0])
    sent(qb, red_send.at[1])
    sent(agg.at[pl.ds(0, 7)], agg_send)
    sent(grad_all.at[:, pl.ds(0, 7 * width)], col_send)
    sent(prod_in.at[pl.ds(0, nr - 1)], prod_send)
    sent(stats_y.at[pl.ds(0, NY - 1)], stat_send.at[0])
    sent(stats.at[pl.ds(0, nz - 1)], stat_send.at[1])
    sent(term_in.at[pl.ds(0, NY - 1)], term_send.at[0])
    sent(term_last.at[pl.ds(0, nz - 1)], term_send.at[1])


def write_kernel(*refs):
    n = len(refs) // 2
    for i in range(n):
        refs[n + i][...] = refs[i][...]


def body(
    features,
    node_order,
    adj_tiles,
    counts,
    coords,
    w_self,
    w_neigh,
    norm_gain,
    norm_bias,
    mean_scale,
    cotangent,
):
    nb, nr = lax.axis_size("blk"), lax.axis_size("rep")
    rows_blk, wide = features.shape
    width = cotangent.shape[1]
    rows = rows_blk // nr
    thin = wide // nb
    steps = nb // nr
    nz = nb // NY
    reach = nz // 2
    tiles = adj_tiles[0, 0]
    dma = pltpu.SemaphoreType.DMA
    vmem = pl.BlockSpec(memory_space=pltpu.VMEM)
    smem = pl.BlockSpec(memory_space=pltpu.SMEM)
    hbm = pl.BlockSpec(memory_space=pl.ANY)

    def room(*shape, dtype=BF16):
        return pltpu.VMEM(shape, dtype)

    outs = tuple(
        pl.pallas_call(
            layer_kernel,
            out_shape=(
                jax.ShapeDtypeStruct((rows_blk, width), BF16),
                jax.ShapeDtypeStruct((rows, wide), BF16),
                jax.ShapeDtypeStruct((thin, width), F32),
                jax.ShapeDtypeStruct((3, width), F32),
            ),
            in_specs=[hbm, vmem, hbm, smem, smem, hbm, hbm, vmem, vmem, vmem, vmem],
            out_specs=(vmem,) * 4,
            scratch_shapes=[
                room(rows_blk, wide),
                room(*tiles.shape),
                room(wide, wide),
                room(wide, wide),
                dma((4,)),
                room(NX, ROW_TILE, wide),
                room(steps, rows_blk, rows_blk),
                room(NX, ROW_TILE, width, dtype=F32),
                room(nb, rows, wide),
                room(steps, NX, ROW_TILE, wide),
                room(rows_blk, wide, dtype=F32),
                room(NX, rows, wide),
                room(NX, rows, wide),
                room(NX - 1, rows, wide),
                room(2, rows, wide),
                room(2, rows // 2, wide),
                room(nr, rows, wide),
                room(nr, rows, width),
                room(nr, rows, width),
                room(rows_blk, width, dtype=F32),
                room(8, width, dtype=F32),
                room(NY, 8, width, dtype=F32),
                room(8, width, dtype=F32),
                room(nz, 8, width, dtype=F32),
                room(rows_blk, width),
                room(rows_blk, wide),
                room(rows_blk, wide),
                room(rows, wide, dtype=F32),
                room(NY, nz, thin, width),
                room(NY, nz, thin, width),
                room(nz, thin, width),
                room(nz, thin, width),
                room(steps, NX, ROW_TILE, wide),
                room(nb, rows, wide),
                room(2, reach, rows, wide),
                room(2, nz, rows, wide),
                room(2, nz, rows // 2, wide),
                room(2, ROW_TILE, wide),
                room(2, rows, wide),
                room(ROW_TILE, wide),
                room(2, rows, wide),
                dma((nz + 1,)),
                dma((4, nz)),
                dma((2,)),
                dma((5,)),
                dma(()),
                dma(()),
                dma((steps,)),
                dma((steps,)),
                dma((2,)),
                dma((4,)),
                dma((4,)),
                dma(()),
                dma(()),
                dma(()),
                dma((8,)),
                dma((2,)),
                dma((2,)),
                dma(()),
                dma((8,)),
                dma((2,)),
                dma((2,)),
                dma((steps,)),
                dma(()),
                dma((nb,)),
                dma(()),
                dma((2, reach)),
                dma((2, nz)),
                dma((2, nz)),
                dma((2,)),
                dma((5,)),
                dma(()),
                dma((2,)),
            ],
            compiler_params=pltpu.CompilerParams(
                collective_id=0, has_side_effects=True, vmem_limit_bytes=56 << 20
            ),
            name="layer",
        )(
            features,
            node_order.reshape(1, rows_blk),
            tiles,
            counts.reshape(steps),
            coords[0, 0],
            w_self,
            w_neigh,
            norm_gain.reshape(1, width),
            norm_bias.reshape(1, width),
            mean_scale.reshape(1, width),
            cotangent,
        )
    )
    return tuple(
        pl.pallas_call(
            write_kernel,
            out_shape=tuple(jax.ShapeDtypeStruct(o.shape, o.dtype) for o in outs),
            name="write",
        )(*outs)
    )


def solution(mesh):
    in_specs = (
        P("blk", None),
        P("blk"),
        P("blk", "rep", None, None, None, None),
        P("blk", "rep", None),
        P("blk", "rep", None, None, None),
        P(),
        P(),
        P("rep"),
        P("rep"),
        P("rep"),
        P("blk", "rep"),
    )
    out_specs = (P("blk", "rep"), P(("blk", "rep"), None), P("blk", "rep"), P(None, "rep"))
    return jax.shard_map(body, mesh=mesh, in_specs=in_specs, out_specs=out_specs, check_vma=False)
```

```python
import jax
import jax.numpy as jnp
from jax import lax
from jax.experimental import pallas as pl
from jax.experimental.pallas import tpu as pltpu
from jax.sharding import PartitionSpec as P

EPSILON = 1e-05
MESH = pl.DeviceIdType.MESH
NY = 4
NX = 4
BF16 = jnp.bfloat16
F32 = jnp.float32


def remote(src, dst, send_sem, recv_sem, blk, rep):
    return pltpu.make_async_remote_copy(
        src_ref=src,
        dst_ref=dst,
        send_sem=send_sem,
        recv_sem=recv_sem,
        device_id=(blk, rep),
        device_id_type=MESH,
    )


def greet(peers):
    barrier = pltpu.get_barrier_semaphore()
    for blk, rep in peers:
        pl.semaphore_signal(barrier, inc=1, device_id=(blk, rep), device_id_type=MESH)


def greeted(count):
    pl.semaphore_wait(pltpu.get_barrier_semaphore(), count)


class Place:
    def __init__(self):
        self.b = lax.axis_index("blk")
        self.r = lax.axis_index("rep")
        self.nb = lax.axis_size("blk")
        self.nr = lax.axis_size("rep")
        self.nz = self.nb // NY
        self.y = self.b % NY
        self.z = self.b // NY
        self.x = self.r // 2
        self.k = self.r % 2
        self.sib = self.x * 2 + (1 - self.k)

    def block(self, dy, dz):
        return ((self.z + dz + self.nz) % self.nz) * NY + (self.y + dy + NY) % NY

    def across(self, dx):
        return ((self.x + dx) % NX) * 2 + self.k

    def rep_peers(self):
        return [(self.b, (self.r + d) % self.nr) for d in range(1, self.nr)]


ROW_TILE = 128
COL_TILE = 512
BY_FIRST = (((0,), (0,)), ((), ()))
BY_LAST = (((1,), (1,)), ((), ()))


def layer_kernel(
    feat_hbm,
    order_ref,
    tiles_hbm,
    counts_ref,
    coords_ref,
    self_hbm,
    neigh_hbm,
    gain_ref,
    bias_ref,
    scale_ref,
    cot_ref,
    normed_ref,
    out_ref,
    weight_ref,
    norm_ref,
    feat,
    tiles,
    w_self,
    w_neigh,
    load_sem,
    reordered,
    adj,
    self_pre,
    g,
    o,
    acc,
    pb,
    rb1,
    qb,
    rb2,
    rb3,
    agg,
    prod,
    prod_in,
    pre,
    stat,
    stats_y,
    line_stat,
    stats,
    grad_pre,
    grad_all,
    grad_agg,
    self_rows,
    term,
    term_in,
    term_mid,
    term_last,
    cb,
    pbuf,
    zr,
    yr,
    yh,
    qin,
    qside,
    owed,
    lent,
    line_recv,
    side_recv,
    plane_send,
    plane_recv,
    line_send,
    swap_send,
    swap_recv,
    own_sem,
    red_send,
    red_recv1,
    red_recv2,
    prod_send,
    prod_recv,
    agg_send,
    agg_recv,
    stat_send,
    stat_recv,
    col_send,
    col_recv,
    term_send,
    term_recv,
    back_own,
    back_send,
    part_recv,
    back_line,
    z_recv,
    y_recv,
    h_recv,
    chain_send,
    chain_recv,
    lent_send,
    lent_recv,
):
    at = Place()
    b, r, nb, nr, nz = at.b, at.r, at.nb, at.nr, at.nz
    x, k, sib = at.x, at.k, at.sib
    rows, wide = out_ref.shape
    half = rows // 2
    rows_blk = rows * nr
    width = cot_ref.shape[1]
    nodes = rows_blk * nb
    reach = nz // 2
    sides = rows_blk // tiles.shape[-1]
    side = tiles.shape[-1]
    slots = tiles.shape[1]
    steps = nb // nr

    loads = [
        pltpu.make_async_copy(src, dst, load_sem.at[i])
        for i, (src, dst) in enumerate(
            ((feat_hbm, feat), (tiles_hbm, tiles), (self_hbm, w_self), (neigh_hbm, w_neigh))
        )
    ]
    for load in loads:
        load.start()

    def reorder(low):
        ids = lax.broadcasted_iota(jnp.int32, (rows_blk, ROW_TILE), 0)
        want = order_ref[:, pl.ds(pl.multiple_of(low, ROW_TILE), ROW_TILE)]
        pick = jnp.where(ids == want, 1.0, 0.0).astype(BF16)
        return lax.dot_general(pick, feat[...], BY_FIRST, preferred_element_type=F32).astype(BF16)

    peers = [((b + d) % nb, r) for d in range(1, nb)] + at.rep_peers()
    greet(peers)
    loads[0].wait()
    reordered[x] = reorder(x * ROW_TILE)
    g[b] = reordered[x, pl.ds(pl.multiple_of(k * rows, rows), rows), :]
    greeted(len(peers))
    opposite = (x + 2) % NX
    far_blk = nb // steps

    def pass_on(c, sem, blk, low=0, count=rows):
        part = pl.ds(low, count)
        return remote(g.at[c, part], g.at[c, part], line_send, sem, blk, r)

    def hand_out(dy, dz):
        c = at.block(dy, dz)
        diff = (b - c + nb) % nb
        goal = diff % nr
        step = diff // nr
        slot = o.at[step, x, pl.ds(pl.multiple_of(k * rows, rows), rows)]

        @pl.when((goal != r) & (goal // 2 != opposite))
        def _():
            remote(g.at[c], slot, swap_send, swap_recv.at[step], b, goal).start()

        @pl.when(goal == r)
        def _():
            pltpu.make_async_copy(g.at[c], slot, own_sem.at[step]).start()

    def fill_block(step):
        def run():
            if step == 0:
                loads[1].wait()
            for i in range(sides):
                for j in range(sides):
                    block = jnp.zeros((side, side), F32)
                    for t in range(slots):
                        live = (
                            (t < counts_ref[step])
                            & (coords_ref[step, t, 0] == i)
                            & (coords_ref[step, t, 1] == j)
                        )
                        chosen = jnp.where(live, 1.0, 0.0)
                        block = block + chosen * tiles[step, t].astype(F32)
                    adj[step, i * side : (i + 1) * side, j * side : (j + 1) * side] = block.astype(BF16)

        return run

    def fill_rows(d):
        def run():
            n = (x + d) % NX
            if d % 2:
                reordered[n] = reorder(n * ROW_TILE)
            if d == 0:
                loads[2].wait()
            cols = pl.ds(pl.multiple_of(r * width, width), width)
            self_pre[n] = jnp.dot(reordered[n], w_self[:, cols], preferred_element_type=F32)

        return run

    work = [fill_block(step) for step in range(steps)] + [fill_rows(d) for d in range(NX)]

    def slab(step, low=0, count=ROW_TILE):
        return o.at[step, opposite, pl.ds(low, count)]

    def relay(step_from, step_to, sem, blk, low=0, count=ROW_TILE):
        return remote(
            slab(step_from, low, count), slab(step_to, low, count), plane_send.at[0], plane_recv.at[sem], blk, r
        )

    def shift_out():
        return remote(
            reordered.at[opposite], slab(0), plane_send.at[1], plane_recv.at[0], (b + r) % nb, r
        )

    up, down = (b + far_blk) % nb, (b - far_blk + nb) % nb

    def plane_start():
        @pl.when(r != 0)
        def _():
            shift_out().start()

        @pl.when(r == 0)
        def _():
            o[0, opposite] = reordered[opposite]

    def plane_spread():
        @pl.when(r != 0)
        def _():
            shift_out().wait_recv()

        relay(0, 1, 1, up).start()
        relay(0, 3, 3, down).start()

    def plane_far():
        relay(0, 1, 1, up).wait_recv()
        relay(1, 2, 2, up, 0, rows).start()
        relay(0, 3, 3, down).wait_recv()
        relay(3, 2, 4, down, rows, rows).start()

    def plane_end():
        relay(1, 2, 2, up, 0, rows).wait_recv()
        relay(3, 2, 4, down, rows, rows).wait_recv()

    ORDER = [0] + [dz for t in range(1, reach) for dz in (-t, t)] + [reach]

    def column_step(i):
        dz = ORDER[i]
        c = at.block(0, dz)
        if dz == reach:
            for w in range(2):
                pass_on(c, line_recv.at[reach + w], b, w * half, half).wait_recv()
        elif dz:
            pass_on(c, line_recv.at[dz % nz + (dz < 0)], b).wait_recv()
        for w, way in ((0, 1), (1, -1)):
            if dz == 0 or (dz * way < 0 and abs(dz) < reach - 1):
                n = (dz - way) % nz
                pass_on(c, line_recv.at[n + (n > reach)], at.block(0, way)).start()
            elif dz * way == 1 - reach:
                pass_on(c, line_recv.at[reach + w], at.block(0, way), w * half, half).start()
        for w, way in ((0, 1), (1, -1)):
            pass_on(c, side_recv.at[w, i], at.block(way, 0)).start()
        hand_out(0, dz)

    def side_step(i):
        dz = ORDER[i]
        for w, way in ((0, 1), (1, -1)):
            c = at.block(-way, dz)
            pass_on(c, side_recv.at[w, i], b).wait_recv()
            pass_on(c, side_recv.at[2 + w, i], at.block(way, 0), w * half, half).start()
            hand_out(-way, dz)

    def far_step(i):
        dz = ORDER[i]
        c = at.block(2, dz)
        for w in range(2):
            pass_on(c, side_recv.at[2 + w, i], b, w * half, half).wait_recv()
        hand_out(2, dz)

    lag = 2
    for i in range(nz + lag + 1):
        if i < nz:
            column_step(i)
        if i == 0:
            reordered[opposite] = reorder(opposite * ROW_TILE)
            plane_start()
        if lag <= i < nz + lag:
            side_step(i - lag)
        if lag < i:
            far_step(i - lag - 1)
        if i == 4:
            plane_spread()
        if i == 8:
            plane_far()
        if i >= 2:
            if work:
                work.pop(0)()
    plane_end()

    for i, step in enumerate((0, 1, 3, 2)):
        some = o.at[step, 0, pl.ds(0, rows)]
        pltpu.make_async_copy(some, some, own_sem.at[step]).wait()
        some = g.at[pl.ds(0, nr - 3)]
        remote(some, some, swap_send, swap_recv.at[step], b, r).wait_recv()

        def part_tile(n, carry, step=step, i=i):
            cols = pl.ds(pl.multiple_of(n * COL_TILE, COL_TILE), COL_TILE)
            source = o[step, :, :, cols].reshape(rows_blk, COL_TILE)
            out = jnp.dot(adj[step], source, preferred_element_type=F32)
            acc[:, cols] = out if i == 0 else acc[:, cols] + out
            return carry

        lax.fori_loop(0, wide // COL_TILE, part_tile, 0)

    def chunk(m):
        return acc[pl.ds(pl.multiple_of(m * rows, rows), rows), :]

    def to_sibling(m):
        return remote(pb.at[m], rb1.at[m], red_send.at[0], red_recv1.at[m], b, sib)

    def both(m):
        return chunk(k * NX + m) + rb1[m].astype(F32)

    turns = [(x + d) % NX for d in (2, 1, 3, 0)]
    for m in turns:
        pb[m] = chunk((1 - k) * NX + m).astype(BF16)
        to_sibling(m).start()
    loads[3].wait()

    def half_way(w):
        part = pl.ds(w * half, half)
        return remote(
            qb.at[0, part], rb3.at[w], red_send.at[1], red_recv2.at[w], b, at.across((1, 3)[w])
        )

    def one_way(w):
        return remote(
            qb.at[1 + w], rb2.at[w], red_send.at[1], red_recv2.at[2 + w], b, at.across((1, 3)[w])
        )

    to_sibling(turns[0]).wait_recv()
    qb[0] = both(turns[0]).astype(BF16)
    for w in range(2):
        half_way(w).start()
    for w in range(2):
        to_sibling(turns[1 + w]).wait_recv()
        value = both(turns[1 + w])
        qb[1 + w] = value.astype(BF16)
        half_way(w).wait_recv()
        part = pl.ds(w * half, half)
        qb[1 + w, part] = (value[w * half : (w + 1) * half] + rb3[w].astype(F32)).astype(BF16)
        one_way(w).start()
    home = k * NX + x
    to_sibling(x).wait_recv()
    total = both(x)
    for w in range(2):
        one_way(w).wait_recv()
        total = total + rb2[w].astype(F32)
    agg[home] = total.astype(BF16)

    for n in range(wide // COL_TILE):
        cols = slice(n * COL_TILE, (n + 1) * COL_TILE)
        out = jnp.dot(agg[home], w_neigh[:, cols], preferred_element_type=F32)
        for j in range(COL_TILE // width):
            prod[n * (COL_TILE // width) + j] = out[:, j * width : (j + 1) * width].astype(BF16)
    for d in (4, 5, 2, 3, 6, 7, 1):
        goal = (r + d) % nr
        remote(prod.at[goal], prod_in.at[home], prod_send, prod_recv, b, goal).start()
    prod_in[home] = prod[r]

    class Line:
        def __init__(self, ref, tall, send, recv):
            self.ref, self.tall, self.send, self.recv = ref, tall, send, recv

        def move(self, chip, core, sem, goal, low=0, count=None):
            ref = self.ref(chip, core, low, self.tall if count is None else count)
            return remote(ref, ref, self.send, self.recv.at[sem], b, goal)

        def begin(self):
            self.move(x, k, 4, sib).start()
            self.move(x, k, 0, at.across(1)).start()
            self.move(x, k, 1, at.across(3)).start()

        def middle(self):
            side = self.tall // 2
            for w, d in ((0, 3), (1, 1)):
                chip = (x + d) % NX
                self.move(chip, k, w, sib).wait_recv()
                self.move(chip, k, 2 + w, at.across(4 - d), w * side, side).start()
                self.move(chip, k, 5 + w, sib).start()

        def end(self):
            side = self.tall // 2
            chip = (x + 2) % NX
            for w in range(2):
                self.move(chip, k, 2 + w, sib, w * side, side).wait_recv()
            self.move(chip, k, 7, sib).start()

        def wait(self):
            for i, d in enumerate((0, 3, 1, 2)):
                self.move((x + d) % NX, 1 - k, 4 + i, sib).wait_recv()

    def agg_chunk(chip, core, low, count):
        return agg.at[core * NX + chip, pl.ds(low, count)]

    def grad_chunk(chip, core, low, count):
        cols = pl.ds(pl.multiple_of((chip * 2 + core) * width, width), width)
        return grad_all.at[pl.ds(low, count), cols]

    agg_line = Line(agg_chunk, rows, agg_send, agg_recv)
    grad_line = Line(grad_chunk, rows_blk, col_send, col_recv)
    agg_line.begin()
    some = prod_in.at[pl.ds(0, nr - 1)]
    remote(some, some, prod_send, prod_recv, b, sib).wait_recv()

    pre[...] = self_pre[...].reshape(rows_blk, width) + prod_in[...].astype(F32).reshape(
        rows_blk, width
    )
    upstream = cot_ref[...].astype(F32)
    near_mean = jnp.sum(pre[...], axis=0, keepdims=True) / rows_blk
    off = pre[...] - near_mean
    stat[0:1, :] = near_mean
    stat[1:2, :] = jnp.sum(off * off, axis=0, keepdims=True)
    stat[2:3, :] = jnp.sum(upstream, axis=0, keepdims=True)
    stat[3:4, :] = jnp.sum(upstream * off, axis=0, keepdims=True)
    stat[4:8, :] = jnp.zeros((4, width), F32)
    stats_y[at.y] = stat[...]
    for d in (2, 1, 3):
        remote(
            stat, stats_y.at[at.y], stat_send.at[0], stat_recv.at[0], at.block(d, 0), r
        ).start()
    some = stats_y.at[pl.ds(0, NY - 1)]
    remote(some, some, stat_send.at[0], stat_recv.at[0], b, sib).wait_recv()
    line_means, line_cots = stats_y[:, 0, :], stats_y[:, 2, :]
    line_mean = jnp.sum(line_means, axis=0, keepdims=True) / NY
    apart = line_means - line_mean
    line_stat[0:1, :] = line_mean
    line_stat[1:2, :] = jnp.sum(
        stats_y[:, 1, :] + rows_blk * apart * apart, axis=0, keepdims=True
    )
    line_stat[2:3, :] = jnp.sum(line_cots, axis=0, keepdims=True)
    line_stat[3:4, :] = jnp.sum(stats_y[:, 3, :] + line_cots * apart, axis=0, keepdims=True)
    line_stat[4:8, :] = jnp.zeros((4, width), F32)
    stats[at.z] = line_stat[...]
    for d in (4, 3, 5, 2, 6, 1, 7):
        remote(
            line_stat, stats.at[at.z], stat_send.at[1], stat_recv.at[1], at.block(0, d), r
        ).start()
    some = stats.at[pl.ds(0, nz - 1)]
    remote(some, some, stat_send.at[1], stat_recv.at[1], b, sib).wait_recv()

    gain, mean_scale = gain_ref[...], scale_ref[...]
    means, cots = stats[:, 0, :], stats[:, 2, :]
    col_mean = jnp.sum(means, axis=0, keepdims=True) / nz
    moved = means - mean_scale * col_mean
    spread = (
        jnp.sum(stats[:, 1, :] + NY * rows_blk * moved * moved, axis=0, keepdims=True) / nodes
    )
    cot_sum = jnp.sum(cots, axis=0, keepdims=True)
    cot_cent = jnp.sum(stats[:, 3, :] + cots * moved, axis=0, keepdims=True)
    col_scale = jnp.sqrt(spread + EPSILON)
    cube = col_scale * col_scale * col_scale
    sharp = gain / col_scale
    weight = gain * cot_cent / (nodes * cube)
    grad_cent_total = sharp * cot_sum - (1.0 - mean_scale) * col_mean * gain * cot_cent / cube
    centered = pre[...] - mean_scale * col_mean
    grad_pre[...] = (
        sharp * upstream - centered * weight - mean_scale * grad_cent_total / nodes
    ).astype(BF16)

    grad_all[:, pl.ds(pl.multiple_of(r * width, width), width)] = grad_pre[...]
    grad_line.begin()
    normed_ref[...] = (sharp * centered + bias_ref[...]).astype(BF16)
    norm_ref[0:1, :] = cot_cent / col_scale / nodes
    norm_ref[1:2, :] = cot_sum / nodes
    norm_ref[2:3, :] = -col_mean * grad_cent_total / nodes
    agg_line.middle()
    grad_line.middle()
    agg_line.end()
    grad_line.end()
    grad_line.wait()

    def agg_tile(n, carry):
        low = pl.ds(pl.multiple_of(n * COL_TILE, COL_TILE), COL_TILE)
        out = lax.dot_general(
            grad_all[...], w_neigh[low, :], BY_LAST, preferred_element_type=F32
        )
        grad_agg[:, low] = out.astype(BF16)
        return carry

    lax.fori_loop(0, wide // COL_TILE, agg_tile, 0)

    def term_y():
        agg_line.wait()
        thin = weight_ref.shape[0]
        for n in range(wide // COL_TILE):
            cols = slice(n * COL_TILE, (n + 1) * COL_TILE)
            source = agg[:, :, cols].reshape(rows_blk, COL_TILE)
            out = lax.dot_general(source, grad_pre[...], BY_FIRST, preferred_element_type=F32)
            each = COL_TILE // thin
            for j in range(each):
                at_z, at_y = divmod(n * each + j, NY)
                term[at_y, at_z] = out[j * thin : (j + 1) * thin].astype(BF16)
        for d in (2, 1, 3):
            goal = (at.y + d) % NY
            remote(
                term.at[goal], term_in.at[at.y], term_send.at[0], term_recv.at[0], at.block(d, 0), r
            ).start()
        term_in[at.y] = term[at.y]

    def term_z():
        some = term_in.at[pl.ds(0, NY - 1)]
        remote(some, some, term_send.at[0], term_recv.at[0], b, sib).wait_recv()
        term_mid[...] = jnp.sum(term_in[...].astype(F32), axis=0).astype(BF16)
        for d in (4, 3, 5, 2, 6, 1, 7):
            goal = (at.z + d) % nz
            remote(
                term_mid.at[goal], term_last.at[at.z], term_send.at[1], term_recv.at[1], at.block(0, d), r
            ).start()
        term_last[at.z] = term_mid[at.z]

    def owed_slab(step, low=0, count=ROW_TILE):
        return cb.at[step, opposite, pl.ds(low, count)]

    def chain_half(w, blk):
        return remote(
            owed_slab(2, w * rows, rows), qside.at[w], chain_send.at[0], chain_recv.at[w], blk, r
        )

    def chain_whole(w, blk):
        return remote(
            owed_slab((1, 3)[w]), qin.at[w], chain_send.at[0], chain_recv.at[2 + w], blk, r
        )

    def chain_shift():
        return remote(
            owed_slab(0), owed, chain_send.at[1], chain_recv.at[4], (b - r + nb) % nb, r
        )

    near = [sib] + [((x + d) % NX) * 2 + j for d in (1, 3) for j in range(2)]
    for step in (2, 1, 3, 0):

        def back_tile(n, carry, step=step):
            cols = pl.ds(pl.multiple_of(n * COL_TILE, COL_TILE), COL_TILE)
            out = lax.dot_general(
                adj[step], grad_agg[:, cols], BY_FIRST, preferred_element_type=F32
            )
            cb[step, :, :, cols] = out.astype(BF16).reshape(NX, ROW_TILE, COL_TILE)
            return carry

        lax.fori_loop(0, wide // COL_TILE, back_tile, 0)
        c = (b - r - nr * step + 2 * nb) % nb
        for goal in near:
            low = pl.multiple_of(goal % 2 * rows, rows)
            remote(
                cb.at[step, goal // 2, pl.ds(low, rows)], pbuf.at[c], back_send, part_recv.at[c], b, goal
            ).start()
        low = pl.multiple_of(k * rows, rows)
        pltpu.make_async_copy(
            cb.at[step, x, pl.ds(low, rows)], pbuf.at[c], back_own.at[step]
        ).start()
        if step == 2:
            chain_half(0, down).start()
            chain_half(1, up).start()
    term_y()
    own_rows = pl.ds(pl.multiple_of(r * rows, rows), rows)
    self_rows[...] = lax.dot_general(
        grad_all[own_rows, :], w_self[...], BY_LAST, preferred_element_type=F32
    )
    for w, blk in ((0, down), (1, up)):
        step = (1, 3)[w]
        part = pl.ds(w * rows, rows)
        chain_half(w, blk).wait_recv()
        cb[step, opposite, part] = (
            cb[step, opposite, part].astype(F32) + qside[w].astype(F32)
        ).astype(BF16)
        chain_whole(w, blk).start()
    for step in range(steps):
        c = (b - r - nr * step + 2 * nb) % nb
        pltpu.make_async_copy(pbuf.at[c], pbuf.at[c], back_own.at[step]).wait()

    def chain_sum():
        for w, blk in ((0, down), (1, up)):
            chain_whole(w, blk).wait_recv()
        cb[0, opposite] = (
            cb[0, opposite].astype(F32) + qin[0].astype(F32) + qin[1].astype(F32)
        ).astype(BF16)

        @pl.when(r != 0)
        def _():
            chain_shift().start()

        @pl.when(r == 0)
        def _():
            owed[...] = cb[0, opposite]

    def lend(j):
        return remote(
            owed.at[pl.ds(j * rows, rows)], lent.at[k], lent_send, lent_recv.at[k], b, opposite * 2 + j
        )

    def chain_lend():
        @pl.when(r != 0)
        def _():
            chain_shift().wait_recv()

        for j in range(2):
            lend(j).start()

    def own(dy, dz):
        c = at.block(dy, dz)
        source = (b - c + nb) % nr

        @pl.when((source != r) & (source // 2 != opposite))
        def _():
            remote(pbuf.at[c], pbuf.at[c], back_send, part_recv.at[c], b, r).wait_recv()

        @pl.when(source // 2 == opposite)
        def _():
            pbuf[c] = jnp.zeros((rows, wide), BF16)

        return c

    BACK = [reach] + [dz for t in range(reach - 1, 0, -1) for dz in (t, -t)] + [0]

    def back_far(i):
        c = own(2, BACK[i])
        for w, way in ((0, 1), (1, -1)):
            part = pl.ds(w * half, half)
            remote(
                pbuf.at[c, part], yh.at[w, i], back_line, h_recv.at[w, i], at.block(way, 0), r
            ).start()

    def back_side(i):
        for w, way in ((0, 1), (1, -1)):
            c = own(way, BACK[i])
            remote(yh.at[w, i], yh.at[w, i], back_line, h_recv.at[w, i], b, r).wait_recv()
            part = pl.ds(w * half, half)
            pbuf[c, part] = (pbuf[c, part].astype(F32) + yh[w, i].astype(F32)).astype(BF16)
            remote(
                pbuf.at[c], yr.at[w, i], back_line, y_recv.at[w, i], at.block(way, 0), r
            ).start()

    def z_send(c, w, t, low=0, count=rows):
        part = pl.ds(low, count)
        return remote(
            pbuf.at[c, part], zr.at[w, t, part], back_line, z_recv.at[w, t], at.block(0, (1, -1)[w]), r
        )

    def back_column(i):
        dz = BACK[i]
        c = own(0, dz)
        for w in range(2):
            remote(yr.at[w, i], yr.at[w, i], back_line, y_recv.at[w, i], b, r).wait_recv()
        value = pbuf[c].astype(F32) + yr[0, i].astype(F32) + yr[1, i].astype(F32)
        if dz == reach:
            pbuf[c] = value.astype(BF16)
            for w in range(2):
                z_send(c, w, reach - 1, w * half, half).start()
            return None
        if dz == 0:
            for w in range(2):
                z_send(c, w, 0).wait_recv()
                value = value + zr[w, 0].astype(F32)
            return value
        w, t = (0, dz) if dz > 0 else (1, -dz)
        if t == reach - 1:
            low = w * half
            z_send(c, w, t, low, half).wait_recv()
            pbuf[c] = value.astype(BF16)
            part = pl.ds(low, half)
            pbuf[c, part] = (value[low : low + half] + zr[w, t, part].astype(F32)).astype(BF16)
        else:
            z_send(c, w, t).wait_recv()
            pbuf[c] = (value + zr[w, t].astype(F32)).astype(BF16)
        z_send(c, w, t - 1).start()
        return None

    for i in range(nz + 4):
        if i < nz:
            back_far(i)
        if 2 <= i < nz + 2:
            back_side(i - 2)
        if i >= 4:
            value = back_column(i - 4)
        if i == 4:
            chain_sum()
        if i == 5:
            term_z()
        if i == 7:
            chain_lend()
    for j in range(2):
        remote(lent.at[j], lent.at[j], lent_send, lent_recv.at[j], b, r).wait_recv()
        value = value + lent[j].astype(F32)
    out_ref[...] = (value + self_rows[...]).astype(BF16)

    some = term_last.at[pl.ds(0, nz - 1)]
    remote(some, some, term_send.at[1], term_recv.at[1], b, sib).wait_recv()
    weight_ref[...] = jnp.sum(term_last[...].astype(F32), axis=0) / nodes

    def sent(some, sem):
        remote(some, some, sem, term_recv.at[0], b, sib).wait_send()

    sent(g.at[pl.ds(0, 3 + 4 * (nz - 1))], line_send)
    sent(g.at[pl.ds(0, steps * (nr - 3))], swap_send)
    sent(o.at[0, pl.ds(0, NX - 1)], plane_send.at[0])
    sent(cb.at[0, pl.ds(0, NX - 1)], chain_send.at[0])

    @pl.when(r != 0)
    def _():
        shift_out().wait_send()
        chain_shift().wait_send()

    sent(lent, lent_send)
    sent(pbuf.at[pl.ds(0, 3 + 4 * (nz - 1))], back_line)
    sent(pbuf.at[pl.ds(0, steps * (nr - 3))], back_send)
    sent(pb, red_send.at[0])
    sent(qb, red_send.at[1])
    sent(agg.at[pl.ds(0, 7)], agg_send)
    sent(grad_all.at[:, pl.ds(0, 7 * width)], col_send)
    sent(prod_in.at[pl.ds(0, nr - 1)], prod_send)
    sent(stats_y.at[pl.ds(0, NY - 1)], stat_send.at[0])
    sent(stats.at[pl.ds(0, nz - 1)], stat_send.at[1])
    sent(term_in.at[pl.ds(0, NY - 1)], term_send.at[0])
    sent(term_last.at[pl.ds(0, nz - 1)], term_send.at[1])


def write_kernel(*refs):
    n = len(refs) // 2
    for i in range(n):
        refs[n + i][...] = refs[i][...]


def body(
    features,
    node_order,
    adj_tiles,
    counts,
    coords,
    w_self,
    w_neigh,
    norm_gain,
    norm_bias,
    mean_scale,
    cotangent,
):
    nb, nr = lax.axis_size("blk"), lax.axis_size("rep")
    rows_blk, wide = features.shape
    width = cotangent.shape[1]
    rows = rows_blk // nr
    thin = wide // nb
    steps = nb // nr
    nz = nb // NY
    reach = nz // 2
    tiles = adj_tiles[0, 0]
    dma = pltpu.SemaphoreType.DMA
    vmem = pl.BlockSpec(memory_space=pltpu.VMEM)
    smem = pl.BlockSpec(memory_space=pltpu.SMEM)
    hbm = pl.BlockSpec(memory_space=pl.ANY)

    def room(*shape, dtype=BF16):
        return pltpu.VMEM(shape, dtype)

    outs = tuple(
        pl.pallas_call(
            layer_kernel,
            out_shape=(
                jax.ShapeDtypeStruct((rows_blk, width), BF16),
                jax.ShapeDtypeStruct((rows, wide), BF16),
                jax.ShapeDtypeStruct((thin, width), F32),
                jax.ShapeDtypeStruct((3, width), F32),
            ),
            in_specs=[hbm, vmem, hbm, smem, smem, hbm, hbm, vmem, vmem, vmem, vmem],
            out_specs=(vmem,) * 4,
            scratch_shapes=[
                room(rows_blk, wide),
                room(*tiles.shape),
                room(wide, wide),
                room(wide, wide),
                dma((4,)),
                room(NX, ROW_TILE, wide),
                room(steps, rows_blk, rows_blk),
                room(NX, ROW_TILE, width, dtype=F32),
                room(nb, rows, wide),
                room(steps, NX, ROW_TILE, wide),
                room(rows_blk, wide, dtype=F32),
                room(NX, rows, wide),
                room(NX, rows, wide),
                room(NX - 1, rows, wide),
                room(2, rows, wide),
                room(2, rows // 2, wide),
                room(nr, rows, wide),
                room(nr, rows, width),
                room(nr, rows, width),
                room(rows_blk, width, dtype=F32),
                room(8, width, dtype=F32),
                room(NY, 8, width, dtype=F32),
                room(8, width, dtype=F32),
                room(nz, 8, width, dtype=F32),
                room(rows_blk, width),
                room(rows_blk, wide),
                room(rows_blk, wide),
                room(rows, wide, dtype=F32),
                room(NY, nz, thin, width),
                room(NY, nz, thin, width),
                room(nz, thin, width),
                room(nz, thin, width),
                room(steps, NX, ROW_TILE, wide),
                room(nb, rows, wide),
                room(2, reach, rows, wide),
                room(2, nz, rows, wide),
                room(2, nz, rows // 2, wide),
                room(2, ROW_TILE, wide),
                room(2, rows, wide),
                room(ROW_TILE, wide),
                room(2, rows, wide),
                dma((nz + 1,)),
                dma((4, nz)),
                dma((2,)),
                dma((5,)),
                dma(()),
                dma(()),
                dma((steps,)),
                dma((steps,)),
                dma((2,)),
                dma((4,)),
                dma((4,)),
                dma(()),
                dma(()),
                dma(()),
                dma((8,)),
                dma((2,)),
                dma((2,)),
                dma(()),
                dma((8,)),
                dma((2,)),
                dma((2,)),
                dma((steps,)),
                dma(()),
                dma((nb,)),
                dma(()),
                dma((2, reach)),
                dma((2, nz)),
                dma((2, nz)),
                dma((2,)),
                dma((5,)),
                dma(()),
                dma((2,)),
            ],
            compiler_params=pltpu.CompilerParams(
                collective_id=0, has_side_effects=True, vmem_limit_bytes=56 << 20
            ),
            name="layer",
        )(
            features,
            node_order.reshape(1, rows_blk),
            tiles,
            counts.reshape(steps),
            coords[0, 0],
            w_self,
            w_neigh,
            norm_gain.reshape(1, width),
            norm_bias.reshape(1, width),
            mean_scale.reshape(1, width),
            cotangent,
        )
    )
    return tuple(
        pl.pallas_call(
            write_kernel,
            out_shape=tuple(jax.ShapeDtypeStruct(o.shape, o.dtype) for o in outs),
            name="write",
        )(*outs)
    )


def solution(mesh):
    in_specs = (
        P("blk", None),
        P("blk"),
        P("blk", "rep", None, None, None, None),
        P("blk", "rep", None),
        P("blk", "rep", None, None, None),
        P(),
        P(),
        P("rep"),
        P("rep"),
        P("rep"),
        P("blk", "rep"),
    )
    out_specs = (P("blk", "rep"), P(("blk", "rep"), None), P("blk", "rep"), P(None, "rep"))
    return jax.shard_map(body, mesh=mesh, in_specs=in_specs, out_specs=out_specs, check_vma=False)
```
